32 devices in a mesh: groups: 2 (over x), seq: 16 (over z, y, core).
Axes of the slice: x: 2, y: 2, z: 4, core: 2. Of those that a mesh axis runs over, the one named last changes fastest.
Arguments:
- queries: bfloat16 [32, 32, 1024], P('seq', 'groups'), parts along dimension 1, may hold values from -1100 to 1100
- keys: bfloat16 [32, 32, 128], P('seq', 'groups'), parts along dimension 1, may hold values from -4 to 4
- values: bfloat16 [32, 32, 128], P('seq', 'groups'), parts along dimension 1, may hold values from -6 to 6
- cache_keys: bfloat16 [32, 2048, 128], P(('groups', 'seq')), parts along dimension 0, may hold values from -4 to 4
- cache_values: bfloat16 [32, 2048, 128], P(('groups', 'seq')), parts along dimension 0, may hold values from -6 to 6
- cache_len: int32 [32, 16], P(None, 'groups'), parts along dimension 1, may hold values from 1 to 2048, as said below
- out_weight: bfloat16 [2048, 2048], P('seq'), may hold values from -0.5 to 0.5
- norm_gain: bfloat16 [2048], replicated, may hold values from 0.5 to 1.5
- expert_ids: int32 [32, 16, 8], P('seq', 'groups'), parts along dimension 1, may hold values from 0 to 31, all different within a row; in each aligned block of 16 rows (0 to 15, 16 to 31, ..., all dimensions but the last counted through in order) at most 5 rows name the same one
- route_weights: float32 [32, 16, 8], P('seq', 'groups'), parts along dimension 1, may hold values from 0.02 to 1
- w_gate: bfloat16 [32, 2048, 384], P('seq'), may hold values from -0.125 to 0.125
- w_up: bfloat16 [32, 2048, 384], P('seq'), may hold values from -0.125 to 0.125
- w_down: bfloat16 [32, 384, 2048], P('seq'), may hold values from -0.3125 to 0.3125
Outputs:
- projected: bfloat16 [32, 16, 2048], P('seq', 'groups'), parts along dimension 1
- moe_out: bfloat16 [32, 16, 2048], P('seq', 'groups'), parts along dimension 1
The draws below stay inside these ranges and needn't reach their ends.
There are 2 independent parts, one for each index of `groups`. The reference program is written for one: setup_inputs(seed, part) draws one part's arguments, and reference() takes and returns one part's arrays. A program takes and returns all parts, laid end to end along the dimension named above; an argument that names none is the same for every part. Nothing has to cross between parts.
Inputs may be any that keep to these rules, and one draw needn't show every extreme that they name: `cache_len`: every new token sees at least one cached key; some token sees all 2048. `expert_ids`: rows are taken position-major over members; in each aligned block of 16 rows (the rows of one index of seq) no expert is named more than 5 times, a bound that some block reaches.
All inputs are finite; a program needn't handle non-finite values.
Results may differ from the reference program's by a relative error of at most 0.01.
Values may be sent and summed in bfloat16 or wider, within the bound.
No kernel may reach another device: no remote copies, remote signals or barrier semaphores. Data moves between devices by JAX's collectives and lax.ppermute only.
A program may use at most 64 MiB of HBM per device.

```python
import math
import jax
import jax.numpy as jnp
import numpy as np
from jax import lax

D = 2048
HD = 128
TOPK = 8
QH = 16
KVH = 2
MOE_FF = 384
CACHE = 2048
EXPERTS = 32
MEMBERS = 8
SLOTS = 16
NEW = 32
TOK_DEV = 16
CAP = 5
N_SEQ = 16


def paired_heads(key):
    base_key = jax.random.fold_in(key, 11)
    key_draw, query_draw = jax.random.split(base_key, 2)
    keys_f = jnp.clip(jax.random.normal(key_draw, (NEW, SLOTS, HD), jnp.float32), -4.0, 4.0)
    queries_f = jnp.clip(1.5 * jax.random.normal(query_draw, (NEW, SLOTS, QH // KVH, HD), jnp.float32), -9.0, 9.0)
    return (queries_f, keys_f)


def draw_queries(key, part):
    queries_f, keys_f = paired_heads(key)
    return queries_f.reshape(NEW, SLOTS, QH // KVH * HD).astype(jnp.bfloat16)


def draw_keys(key, part):
    queries_f, keys_f = paired_heads(key)
    return keys_f.astype(jnp.bfloat16)


def draw_cache_len(key, part):
    drawn = jax.random.randint(jax.random.fold_in(key, 5), (NEW, MEMBERS), 1, CACHE + 1)
    return drawn.at[0, 0].set(CACHE).astype(jnp.int32)


def level_of(own_key, extent, pieces, low, high):
    factor_of, own = 1.0, jax.random.fold_in(own_key, 6)
    for axis_at, blocks in pieces:
        heights = jnp.exp(jax.random.uniform(jax.random.fold_in(own, axis_at), (blocks,), jnp.float32, low / len(pieces), high / len(pieces)))
        factor_of = factor_of * jnp.repeat(heights, extent[axis_at] // blocks).reshape([-1 if axis == axis_at else 1 for axis in range(len(extent))])
    return factor_of


def assign_block(key, own, number, rows, count, top, bound, slope):
    order = jax.random.permutation(key, count)
    heavy_load, common = portions_of(count, rows * top, bound, slope, True), portions_of(count, rows * top, bound, slope, False)
    places = jnp.arange(count)

    def named(sizes, turn):
        used = int((sizes > 0).sum())
        fixed = max(1, used // 4)
        passed = fixed + (places - fixed + turn * (used - fixed)) % max(1, count - fixed)
        return jnp.zeros((count,), jnp.int32).at[order[jnp.where(places < fixed, places, passed)]].set(jnp.asarray(sizes, jnp.int32))

    sizes = jnp.where(number % 4 == 0, named(heavy_load, number // 4), named(common, number - number // 4 - 1))
    mixed = jax.random.permutation(jax.random.fold_in(own, 3), count)
    giver, sink = mixed[0:count // 2 * 2:2], mixed[1:count // 2 * 2:2]
    slack = jnp.minimum(sizes[giver] - 1, bound - sizes[sink]) // 2
    slack = jnp.where((giver == order[0]) | (sink == order[0]) | (sizes[sink] == 0), 0, jnp.maximum(slack, 0))
    passed = jax.random.randint(jax.random.fold_in(own, 4), (count // 2,), 0, 1 << 20) % (slack + 1)
    sizes = sizes.at[giver].add(-passed).at[sink].add(passed)
    members = jnp.searchsorted(jnp.cumsum(sizes), jnp.arange(rows * top), side="right").astype(jnp.int32)
    table = members.reshape(top, rows).T
    table = table[jax.random.permutation(jax.random.fold_in(own, 1), rows)]
    turn = jax.random.randint(jax.random.fold_in(own, 2), (rows, 1), 0, top)
    return jnp.take_along_axis(table, (jnp.arange(top)[None, :] + turn) % top, axis=1)


def portions_of(amount, total, reach, lean, full):
    loads = [(1 << 20) // math.isqrt(grade ** lean) + 1 for grade in range(1, amount + 1)]
    largest = reach if full else min(reach, max(-(-total // amount), total * loads[0] // sum(loads)))
    least = 1 if total - largest >= amount - 1 else 0
    counts, surplus = [largest] + [least] * (amount - 1), total - largest - least * (amount - 1)
    while surplus > 0:
        movable = [i for i in range(1, amount) if counts[i] < largest] or [i for i in range(1, amount) if counts[i] < reach]
        whole, left = sum([loads[i] for i in movable]), surplus
        for i in movable:
            addition = min(reach - counts[i], max(1, left * loads[i] // whole), surplus)
            counts[i] = counts[i] + addition
            surplus = surplus - addition
    return np.array(counts)


def normal_values(own_key, dims, deviation, most, pieces=(), kind=jnp.bfloat16):
    entries = jax.random.normal(own_key, dims, jnp.float32) * deviation
    if len(pieces) > 0:
        entries = level_of(own_key, dims, pieces, -0.22, 0.18) * entries
    return jnp.clip(entries, min=-most, max=most).astype(kind)


def setup_inputs(seed: int = 0, part: int = 0) -> dict:
    arg_keys = jax.random.split(jax.random.key(seed), 14)
    part_keys = jax.random.split(jax.random.fold_in(arg_keys[13], part), 14)
    queries = draw_queries(jax.random.fold_in(jax.random.fold_in(arg_keys[13], part), 71), part)
    keys = draw_keys(jax.random.fold_in(jax.random.fold_in(arg_keys[13], part), 71), part)
    values = normal_values(part_keys[2], (NEW, SLOTS, HD), 1.0, 6.0, ((0, 16),))
    cache_keys = normal_values(part_keys[3], (SLOTS, CACHE, HD), 1.0, 4.0, ((0, 16),))
    cache_values = normal_values(part_keys[4], (SLOTS, CACHE, HD), 1.0, 6.0, ((0, 16),))
    cache_len = draw_cache_len(jax.random.fold_in(jax.random.fold_in(arg_keys[13], part), 71), part)
    out_weight = normal_values(arg_keys[6], (QH * HD, D), (QH * HD // 16) ** -0.5, 0.5, ((0, 16),))
    norm_gain = jnp.clip(1.0 + 0.1 * jax.random.normal(arg_keys[7], (D,), jnp.float32), 0.5, 1.5).astype(jnp.bfloat16)
    expert_ids_keys = jax.random.split(jax.random.fold_in(part_keys[8], 1), NEW * MEMBERS // TOK_DEV)
    expert_ids_turns = jax.random.permutation(jax.random.fold_in(part_keys[8], 3), NEW * MEMBERS // TOK_DEV)
    expert_ids = jax.vmap(lambda own, number: assign_block(jax.random.fold_in(part_keys[8], 2), own, number, TOK_DEV, EXPERTS, TOPK, CAP, 2))(expert_ids_keys, expert_ids_turns).reshape((NEW, MEMBERS, TOPK))
    route_weights = jnp.clip(jnp.exp(math.log(1.0) - 3.912023 * jax.random.uniform(part_keys[9], (NEW, MEMBERS, TOPK), jnp.float32) ** level_of(part_keys[9], (NEW, MEMBERS, TOPK), ((0, 16),), -0.2, 0.2)), 0.02, 1.0)
    w_gate = normal_values(arg_keys[10], (EXPERTS, D, MOE_FF), D ** -0.5, 0.125, ((0, 16),))
    w_up = normal_values(arg_keys[11], (EXPERTS, D, MOE_FF), D ** -0.5, 0.125, ((0, 16),))
    w_down = normal_values(arg_keys[12], (EXPERTS, MOE_FF, D), MOE_FF ** -0.5, 0.3125, ((0, 16),))
    return {"queries": queries, "keys": keys, "values": values, "cache_keys": cache_keys, "cache_values": cache_values, "cache_len": cache_len, "out_weight": out_weight, "norm_gain": norm_gain, "expert_ids": expert_ids, "route_weights": route_weights, "w_gate": w_gate, "w_up": w_up, "w_down": w_down}


def attend(inputs):
    query_heads, key_rows, value_rows, lengths = inputs
    new_count = query_heads.shape[0]
    cache_count = key_rows.shape[0] - new_count
    scores = jnp.einsum('qhd,kd->hqk', query_heads.astype(jnp.float32), key_rows.astype(jnp.float32)) * HD ** (-0.5)
    cached_ok = jnp.arange(cache_count, dtype=jnp.int32)[None, :] < lengths[:, None]
    causal_ok = jnp.arange(new_count, dtype=jnp.int32)[None, :] <= jnp.arange(new_count, dtype=jnp.int32)[:, None]
    visible = jnp.concatenate([cached_ok, causal_ok], axis=1)
    scores = jnp.where(visible[None], scores, -1e+30)
    row_max = lax.optimization_barrier(jnp.max(scores, axis=-1, keepdims=True))
    expo = jnp.exp(scores - row_max)
    row_sum = lax.optimization_barrier(jnp.sum(expo, axis=-1, keepdims=True))
    weights = (expo / row_sum).astype(jnp.bfloat16)
    result = jnp.einsum('hqk,kd->qhd', weights.astype(jnp.float32), value_rows.astype(jnp.float32))
    return result.astype(jnp.bfloat16).reshape(new_count, -1)

def reference(queries, keys, values, cache_keys, cache_values, cache_len, out_weight, norm_gain, expert_ids, route_weights, w_gate, w_up, w_down):
    group_q = QH // KVH
    query_slots = jnp.transpose(queries.reshape(NEW, SLOTS, group_q, HD), (1, 0, 2, 3))
    key_slots = jnp.concatenate([cache_keys, jnp.transpose(keys, (1, 0, 2))], axis=1)
    value_slots = jnp.concatenate([cache_values, jnp.transpose(values, (1, 0, 2))], axis=1)
    length_slots = jnp.repeat(jnp.transpose(cache_len), KVH, axis=0)
    attended = lax.map(attend, (query_slots, key_slots, value_slots, length_slots))
    head_rows = jnp.transpose(attended.reshape(MEMBERS, KVH, NEW, group_q * HD), (2, 0, 1, 3)).reshape(NEW * MEMBERS, QH * HD)
    projected = jnp.dot(head_rows, out_weight, preferred_element_type=jnp.float32).astype(jnp.bfloat16)
    flat_rows = projected.astype(jnp.float32)
    stats = lax.optimization_barrier(jnp.mean(flat_rows * flat_rows, axis=-1, keepdims=True))
    normed = (flat_rows * lax.rsqrt(stats + 1e-06) * norm_gain.astype(jnp.float32)).astype(jnp.bfloat16)
    chosen_ids = expert_ids.reshape(NEW * MEMBERS, TOPK)
    raw_weights = route_weights.reshape(NEW * MEMBERS, TOPK)
    norm_weights = raw_weights / lax.optimization_barrier(jnp.sum(raw_weights, axis=1, keepdims=True))
    limit = N_SEQ * CAP

    def one_expert(running, expert):
        chosen = chosen_ids == expert
        shares = lax.optimization_barrier(jnp.sum(jnp.where(chosen, norm_weights, 0.0), axis=1))
        taken = jnp.any(chosen, axis=1)
        chosen_count = jnp.sum(taken.astype(jnp.int32))
        picked = jnp.nonzero(taken, size=limit, fill_value=0)[0].astype(jnp.int32)
        valid = (jnp.arange(limit, dtype=jnp.int32) < chosen_count).astype(jnp.float32)
        row_block = normed[picked]
        gate_out = jnp.dot(row_block, w_gate[expert], preferred_element_type=jnp.float32)
        up_out = jnp.dot(row_block, w_up[expert], preferred_element_type=jnp.float32)
        hidden_act = (jax.nn.silu(gate_out) * up_out).astype(jnp.bfloat16)
        expert_out = jnp.dot(hidden_act, w_down[expert], preferred_element_type=jnp.float32).astype(jnp.bfloat16)
        scaled = expert_out.astype(jnp.float32) * (shares[picked] * valid)[:, None]
        return (running.at[picked].add(scaled), None)
    mixed, unused = lax.scan(one_expert, jnp.zeros((NEW * MEMBERS, D), jnp.float32), jnp.arange(EXPERTS, dtype=jnp.int32))
    moe_out = mixed.astype(jnp.bfloat16).reshape(NEW, MEMBERS, D)
    return (projected.reshape(NEW, MEMBERS, D), moe_out)
```

```python
import functools
import math

import jax
import jax.numpy as jnp
from jax import lax
from jax.experimental import pallas as pl
from jax.experimental.pallas import tpu as pltpu
from jax.sharding import PartitionSpec as P

D = 2048
HD = 128
TOPK = 8
QH = 16
KVH = 2
CAP = 5
LANES = 128

VMEM = pl.BlockSpec(memory_space=pltpu.VMEM)
SMEM = pl.BlockSpec(memory_space=pltpu.SMEM)


def iota(shape, dim):
    return lax.broadcasted_iota(jnp.int32, shape, dim)


def call(kernel, outs, args, scratch=(), vmem_mib=24, flops=0, moved=0):
    return pl.pallas_call(
        kernel,
        out_shape=tuple(jax.ShapeDtypeStruct(s, d) for s, d in outs),
        in_specs=[SMEM if a.ndim == 1 else VMEM for a in args],
        out_specs=tuple(VMEM for _ in outs),
        scratch_shapes=list(scratch),
        compiler_params=pltpu.CompilerParams(vmem_limit_bytes=vmem_mib << 20),
        cost_estimate=pl.CostEstimate(flops=flops, bytes_accessed=moved, transcendentals=0),
    )(*args)


def attend_kernel(at_ref, row_ref, key_ref, value_ref, length_ref, out_ref, score_ref):
    new, heads = row_ref.shape[0], QH // KVH
    wide = heads * HD
    cached = key_ref.shape[1]
    step = math.gcd(cached, 512)
    me = at_ref[0]
    member, group = me // KVH, me % KVH
    length = jnp.sum(
        jnp.where(iota(length_ref.shape, 1) == member, length_ref[...], 0).astype(jnp.float32),
        axis=1,
        keepdims=True,
    ).astype(jnp.int32)
    lengths = jnp.concatenate([length] * heads, axis=0)
    query = jnp.concatenate([row_ref[:, h * HD : (h + 1) * HD] for h in range(heads)], axis=0)
    rows = heads * new
    dims = (((1,), (1,)), ((), ()))
    fresh = lax.dot_general(
        query, row_ref[:, wide : wide + HD], dims, preferred_element_type=jnp.float32
    )
    causal = iota((new, new), 1) <= iota((new, new), 0)
    fresh = jnp.where(jnp.concatenate([causal] * heads, axis=0), fresh, -1e30)
    best = jnp.max(fresh, axis=1, keepdims=True)
    peak = jnp.full((rows, LANES), -1e30, jnp.float32)
    for at in range(0, cached, step):
        part = lax.dot_general(
            query, key_ref[0, at : at + step, :], dims, preferred_element_type=jnp.float32
        )
        part = jnp.where(iota((rows, step), 1) + at < lengths, part, -1e30)
        score_ref[:, at : at + step] = part
        for lane in range(0, step, LANES):
            peak = jnp.maximum(peak, part[:, lane : lane + LANES])
    best = jnp.maximum(best, jnp.max(peak, axis=1, keepdims=True))
    factor = HD ** (-0.5) * math.log2(math.e)
    expo = jnp.exp2((fresh - best) * factor)
    total = jnp.sum(expo, axis=1, keepdims=True)
    result = jnp.dot(
        expo.astype(jnp.bfloat16),
        row_ref[:, wide + HD : wide + 2 * HD],
        preferred_element_type=jnp.float32,
    )
    sums = jnp.zeros((rows, LANES), jnp.float32)
    for at in range(0, cached, step):
        expo = jnp.exp2((score_ref[:, at : at + step] - best) * factor)
        for lane in range(0, step, LANES):
            sums = sums + expo[:, lane : lane + LANES]
        result = result + jnp.dot(
            expo.astype(jnp.bfloat16),
            value_ref[0, at : at + step, :],
            preferred_element_type=jnp.float32,
        )
    total = total + jnp.sum(sums, axis=1, keepdims=True)
    result = (result / total).astype(jnp.bfloat16)
    owned = out_ref.shape[2]
    holders = wide // owned
    out_ref[...] = jnp.zeros(out_ref.shape, out_ref.dtype)
    per = owned // HD
    for d in range(holders):
        for i in range(per):
            h = d * per + i
            out_ref[group * holders + d, :, i * HD : (i + 1) * HD] = result[h * new : (h + 1) * new]


def token_of(at, count, per_dev, per_rows, members, dim, shape):
    r = iota(shape, dim)
    half = count // 2
    odd = r // half
    rest = r % half
    block = (2 * (rest // per_dev) + odd) ^ at
    tok = rest % per_dev
    return block * per_rows + tok // members, tok % members


def project_kernel(per_rows, members, at_ref, head_ref, weight_ref, keep_ref, send_ref):
    count, new, owned = head_ref.shape
    me = at_ref[0]
    group = (me * owned) // (QH // KVH * HD)
    rows = members * new
    head = jnp.concatenate([head_ref[KVH * m + group] for m in range(members)], axis=0)
    position, member = token_of(me, rows, per_rows * members, per_rows, members, 0, (rows, rows))
    pick = (iota((rows, rows), 1) == member * new + position).astype(jnp.bfloat16)
    ordered = jnp.dot(pick, head, preferred_element_type=jnp.float32).astype(jnp.bfloat16)
    half = rows // 2
    step = 512
    for at in range(0, weight_ref.shape[1], step):
        part = jnp.dot(
            ordered, weight_ref[:, at : at + step], preferred_element_type=jnp.float32
        ).astype(jnp.bfloat16)
        keep_ref[:, at : at + step] = part[:half]
        send_ref[:, at : at + step] = part[half:]


def norm_kernel(*refs):
    pieces, (gain_ref, projected_ref, normed_ref) = refs[:-3], refs[-3:]
    total = pieces[0][...].astype(jnp.float32)
    for piece in pieces[1:]:
        total = total + piece[...].astype(jnp.float32)
    projected = total.astype(jnp.bfloat16)
    projected_ref[...] = projected
    flat = projected.astype(jnp.float32)
    stats = jnp.mean(flat * flat, axis=1, keepdims=True)
    normed_ref[...] = (
        flat * lax.rsqrt(stats + 1e-06) * gain_ref[...].astype(jnp.float32)
    ).astype(jnp.bfloat16)


def expert_kernel(
    per_rows, members, at_ref, even_ref, odd_ref, info_ref, gate_ref, up_ref, down_ref, keep_ref, send_ref
):
    me = at_ref[0]
    half = even_ref.shape[0]
    rows = 2 * half
    new = info_ref.shape[0]
    experts = gate_ref.shape[0]
    width = info_ref.shape[1] // 3
    position, _ = token_of(me, rows, per_rows * members, per_rows, members, 0, (rows, new))
    spread = (iota((rows, new), 1) == position).astype(jnp.bfloat16)
    info = jnp.dot(spread, info_ref[...], preferred_element_type=jnp.float32)
    _, member = token_of(me, rows, per_rows * members, per_rows, members, 0, (rows, width))
    mine = iota((rows, width), 1) // TOPK == member
    share = jnp.where(mine, info[:, width : 2 * width] + info[:, 2 * width :], 0.0)
    whole = jnp.sum(share, axis=1, keepdims=True)
    normed = jnp.concatenate([even_ref[...], odd_ref[...]], axis=0)
    hidden = []
    for e in range(experts):
        chosen = info[:, :width] == (me * experts + e).astype(jnp.float32)
        scale = jnp.sum(jnp.where(chosen, share, 0.0), axis=1, keepdims=True) / whole
        gate = jnp.dot(normed, gate_ref[e], preferred_element_type=jnp.float32)
        up = jnp.dot(normed, up_ref[e], preferred_element_type=jnp.float32)
        hidden.append((gate / (1.0 + jnp.exp(-gate)) * up * scale).astype(jnp.bfloat16))
    step = 512
    for at in range(0, down_ref.shape[2], step):
        part = jnp.zeros((rows, step), jnp.float32)
        for e in range(experts):
            part = part + jnp.dot(
                hidden[e], down_ref[e, :, at : at + step], preferred_element_type=jnp.float32
            )
        part = part.astype(jnp.bfloat16)
        keep_ref[:, at : at + step] = part[:half]
        send_ref[:, at : at + step] = part[half:]


def swap(value, offset):
    count = lax.axis_size("seq")
    return lax.ppermute(value, "seq", [(i, i ^ offset) for i in range(count)])


def scatter_pieces(keep, send, per_dev):
    chips = keep.shape[0] // per_dev
    paired = keep + swap(send, 1)
    blocks = [paired[k * per_dev : (k + 1) * per_dev] for k in range(chips)]
    return [blocks[0]] + [swap(blocks[k], 2 * k) for k in range(1, chips)]


def gather_rows(own):
    count = lax.axis_size("seq")
    near = [own] + [swap(own, k) for k in range(4, count, 4)]
    far = [swap(piece, 2) for piece in near]
    even = jnp.concatenate([p for pair in zip(near, far) for p in pair], axis=0)
    return even, swap(even, 1)


def exchange_body(
    queries,
    keys,
    values,
    cache_keys,
    cache_values,
    cache_len,
    out_weight,
    norm_gain,
    expert_ids,
    route_weights,
    w_gate,
    w_up,
    w_down,
):
    count = lax.axis_size("seq")
    per_rows, members = queries.shape[0], count // KVH
    new = per_rows * count
    per_dev = per_rows * members
    rows = per_dev * count
    owned = out_weight.shape[0]
    at = lax.axis_index("seq").astype(jnp.int32).reshape(1)
    picks = members * TOPK
    width = -(-picks // LANES) * LANES
    pad = ((0, 0), (0, width - picks))
    ids = jnp.pad(expert_ids.reshape(per_rows, picks).astype(jnp.bfloat16), pad)
    shares = jnp.pad(route_weights.reshape(per_rows, picks), pad)
    high = lax.reduce_precision(shares, 8, 7)
    low = (shares - high).astype(jnp.bfloat16)
    info = jnp.concatenate([ids, high.astype(jnp.bfloat16), low], axis=1)
    info = jnp.broadcast_to(info[:, None, :], (per_rows, count, 3 * width))
    sent = jnp.concatenate([queries, keys, values, info], axis=2)
    taken = lax.all_to_all(sent, "seq", split_axis=1, concat_axis=0, tiled=True)
    taken = taken.reshape(new, sent.shape[2])
    wide = QH // KVH * HD
    row_count = QH // KVH * new
    (heads,) = call(
        attend_kernel,
        [((count, new, owned), jnp.bfloat16)],
        (at, taken, cache_keys, cache_values, cache_len),
        scratch=[pltpu.VMEM((row_count, cache_keys.shape[1]), jnp.float32)],
        flops=4 * row_count * cache_keys.shape[1] * HD,
        moved=4 * cache_keys.shape[1] * HD,
    )
    heads = lax.all_to_all(heads, "seq", split_axis=0, concat_axis=0, tiled=True)
    keep, send = call(
        functools.partial(project_kernel, per_rows, members),
        [((rows // 2, D), jnp.bfloat16)] * 2,
        (at, heads, out_weight),
        flops=2 * rows * owned * D,
        moved=2 * owned * D,
    )
    pieces = scatter_pieces(keep, send, per_dev)
    projected, normed = call(
        norm_kernel,
        [((per_dev, D), jnp.bfloat16)] * 2,
        (*pieces, norm_gain.reshape(1, D)),
        moved=2 * per_dev * D * (len(pieces) + 2),
    )
    even, odd = gather_rows(normed)
    keep, send = call(
        functools.partial(expert_kernel, per_rows, members),
        [((rows // 2, D), jnp.bfloat16)] * 2,
        (at, even, odd, taken[:, wide + 2 * HD :], w_gate, w_up, w_down),
        vmem_mib=32,
        flops=6 * rows * w_gate.size,
        moved=6 * w_gate.size,
    )
    pieces = scatter_pieces(keep, send, per_dev)
    mixed = sum(piece.astype(jnp.float32) for piece in pieces)
    shape = (per_rows, members, D)
    return (projected.reshape(shape), mixed.astype(jnp.bfloat16).reshape(shape))


def fits(mesh, out_rows, positions, experts):
    count = mesh.shape["seq"]
    owned = out_rows // count
    per_dev = positions // count * (count // KVH)
    power = count & (count - 1) == 0 and count >= 8
    small = per_dev * count * D * 2 <= 2 << 20
    return power and owned % HD == 0 and per_dev % 16 == 0 and positions % 16 == 0 and small and experts <= 256


def attend(query_heads, key_rows, value_rows, lengths):
    new_count = query_heads.shape[0]
    cache_count = key_rows.shape[0] - new_count
    scores = jnp.einsum(
        "qhd,kd->hqk", query_heads, key_rows, preferred_element_type=jnp.float32
    ) * HD ** (-0.5)
    cached_ok = jnp.arange(cache_count, dtype=jnp.int32)[None, :] < lengths[:, None]
    causal_ok = (
        jnp.arange(new_count, dtype=jnp.int32)[None, :]
        <= jnp.arange(new_count, dtype=jnp.int32)[:, None]
    )
    visible = jnp.concatenate([cached_ok, causal_ok], axis=1)
    scores = jnp.where(visible[None], scores, -1e30)
    row_max = jnp.max(scores, axis=-1, keepdims=True)
    expo = jnp.exp(scores - row_max)
    row_sum = jnp.sum(expo, axis=-1, keepdims=True)
    weights = (expo / row_sum).astype(jnp.bfloat16)
    result = jnp.einsum("hqk,kd->qhd", weights, value_rows, preferred_element_type=jnp.float32)
    return result.astype(jnp.bfloat16).reshape(new_count, -1)


def plain_body(
    queries,
    keys,
    values,
    cache_keys,
    cache_values,
    cache_len,
    out_weight,
    norm_gain,
    expert_ids,
    route_weights,
    w_gate,
    w_up,
    w_down,
):
    slot_count = lax.axis_size("seq")
    per_rows = queries.shape[0]
    members = slot_count // KVH
    group_q = QH // KVH
    new_count = per_rows * slot_count
    position_index = lax.axis_index("seq")
    member = position_index // KVH
    query_rows, key_new, value_new = (
        lax.all_to_all(queries, "seq", split_axis=1, concat_axis=0, tiled=True),
        lax.all_to_all(keys, "seq", split_axis=1, concat_axis=0, tiled=True),
        lax.all_to_all(values, "seq", split_axis=1, concat_axis=0, tiled=True),
    )
    key_rows = jnp.concatenate([cache_keys[0], key_new.reshape(new_count, HD)], axis=0)
    value_rows = jnp.concatenate([cache_values[0], value_new.reshape(new_count, HD)], axis=0)
    lengths = lax.dynamic_slice_in_dim(cache_len, member, 1, 1)[:, 0]
    attended = attend(query_rows.reshape(new_count, group_q, HD), key_rows, value_rows, lengths)
    returned_heads = lax.all_to_all(
        attended[:, None, :], "seq", split_axis=0, concat_axis=1, tiled=True
    )
    token_heads = returned_heads.reshape(per_rows * members, QH * HD)
    projected_f = jnp.dot(
        token_heads,
        lax.all_gather(out_weight, "seq", axis=0, tiled=True),
        preferred_element_type=jnp.float32,
    )
    projected_f = projected_f.reshape(per_rows, members, D)
    projected = projected_f.astype(jnp.bfloat16)
    token_count = per_rows * members
    flat_rows = projected.reshape(token_count, D).astype(jnp.float32)
    stats = jnp.mean(flat_rows * flat_rows, axis=-1, keepdims=True)
    normed = (flat_rows * lax.rsqrt(stats + 1e-06) * norm_gain.astype(jnp.float32)).astype(
        jnp.bfloat16
    )
    exp_dev = w_gate.shape[0]
    expert_count = exp_dev * slot_count
    chosen_ids = expert_ids.reshape(token_count * TOPK)
    onehot = (chosen_ids[:, None] == jnp.arange(expert_count, dtype=jnp.int32)[None, :]).astype(
        jnp.int32
    )
    slot_rank = jnp.sum((jnp.cumsum(onehot, axis=0) - onehot) * onehot, axis=1)
    owner = chosen_ids // exp_dev
    local_expert = chosen_ids % exp_dev
    slot_target = (local_expert * slot_count + owner) * CAP + slot_rank
    total_slots = exp_dev * slot_count * CAP
    token_of = jnp.arange(token_count * TOPK, dtype=jnp.int32) // TOPK
    source_row = jnp.full((total_slots,), -1, jnp.int32).at[slot_target].set(token_of)
    filled = source_row >= 0
    outgoing = jnp.where(
        filled[:, None], normed[jnp.maximum(source_row, 0)], jnp.zeros((), jnp.bfloat16)
    )
    outgoing = outgoing.reshape(exp_dev, slot_count, CAP, D)
    incoming = lax.all_to_all(outgoing, "seq", split_axis=1, concat_axis=1, tiled=True)
    row_block = incoming.reshape(exp_dev, slot_count * CAP, D)
    gate_out = jnp.einsum("ecd,edf->ecf", row_block, w_gate, preferred_element_type=jnp.float32)
    up_out = jnp.einsum("ecd,edf->ecf", row_block, w_up, preferred_element_type=jnp.float32)
    hidden_act = (jax.nn.silu(gate_out) * up_out).astype(jnp.bfloat16)
    expert_out = jnp.einsum(
        "ecf,efd->ecd", hidden_act, w_down, preferred_element_type=jnp.float32
    ).astype(jnp.bfloat16)
    expert_back = lax.all_to_all(
        expert_out.reshape(exp_dev, slot_count, CAP, D),
        "seq",
        split_axis=1,
        concat_axis=1,
        tiled=True,
    )
    picked = expert_back.reshape(total_slots, D)[slot_target].reshape(token_count, TOPK, D)
    raw_weights = route_weights.reshape(token_count, TOPK)
    norm_weights = raw_weights / jnp.sum(raw_weights, axis=1, keepdims=True)
    mixed = jnp.sum(norm_weights[:, :, None] * picked.astype(jnp.float32), axis=1)
    moe_out = mixed.astype(jnp.bfloat16).reshape(per_rows, members, D)
    return (projected, moe_out)


def solution(mesh):
    def run(*args):
        chosen = exchange_body if fits(mesh, args[6].shape[0], args[0].shape[0], args[10].shape[0]) else plain_body
        return jax.shard_map(
            chosen,
            mesh=mesh,
            in_specs=(
                P("seq", "groups", None),
                P("seq", "groups", None),
                P("seq", "groups", None),
                P(("groups", "seq"), None, None),
                P(("groups", "seq"), None, None),
                P(None, "groups"),
                P("seq", None),
                P(),
                P("seq", "groups", None),
                P("seq", "groups", None),
                P("seq", None, None),
                P("seq", None, None),
                P("seq", None, None),
            ),
            out_specs=(P("seq", "groups", None), P("seq", "groups", None)),
            check_vma=False,
        )(*args)

    return run
```

```python
import functools
import math

import jax
import jax.numpy as jnp
from jax import lax
from jax.experimental import pallas as pl
from jax.experimental.pallas import tpu as pltpu
from jax.sharding import PartitionSpec as P

D = 2048
HD = 128
TOPK = 8
QH = 16
KVH = 2
CAP = 5
LANES = 128

VMEM = pl.BlockSpec(memory_space=pltpu.VMEM)
SMEM = pl.BlockSpec(memory_space=pltpu.SMEM)


def iota(shape, dim):
    return lax.broadcasted_iota(jnp.int32, shape, dim)


def call(kernel, outs, args, scratch=(), vmem_mib=24, flops=0, moved=0):
    return pl.pallas_call(
        kernel,
        out_shape=tuple(jax.ShapeDtypeStruct(s, d) for s, d in outs),
        in_specs=[SMEM if a.ndim == 1 else VMEM for a in args],
        out_specs=tuple(VMEM for _ in outs),
        scratch_shapes=list(scratch),
        compiler_params=pltpu.CompilerParams(vmem_limit_bytes=vmem_mib << 20),
        cost_estimate=pl.CostEstimate(flops=flops, bytes_accessed=moved, transcendentals=0),
    )(*args)


def pack_kernel(query_ref, key_ref, value_ref, id_ref, share_ref, out_ref):
    per_rows, count, wide = query_ref.shape
    members = id_ref.shape[1]
    width = (out_ref.shape[2] - wide - 2 * HD) // 3
    lane = iota((members, width), 1)
    home = lane // TOPK == iota((members, width), 0)

    def flat(table):
        total = jnp.zeros((members, width), jnp.float32)
        for k in range(TOPK):
            total = jnp.where(home & (lane % TOPK == k), table[:, k : k + 1], total)
        row = jnp.sum(total, axis=0, keepdims=True)
        return jnp.broadcast_to(row, (count, width)).astype(jnp.bfloat16)

    for i in range(per_rows):
        out_ref[i, :, :wide] = query_ref[i]
        out_ref[i, :, wide : wide + HD] = key_ref[i]
        out_ref[i, :, wide + HD : wide + 2 * HD] = value_ref[i]
        share = share_ref[i]
        high = share.astype(jnp.bfloat16).astype(jnp.float32)
        at = wide + 2 * HD
        for table in (id_ref[i].astype(jnp.float32), high, share - high):
            out_ref[i, :, at : at + width] = flat(table)
            at += width


def split_kernel(at_ref, weight_ref, *out_refs):
    me = at_ref[0]
    for k, out_ref in enumerate(out_refs):
        for y in range(2):
            for c in range(2):
                start = pl.multiple_of((me ^ (4 * k + 2 * y + c)) * LANES, LANES)
                out_ref[y, c] = weight_ref[:, pl.ds(start, LANES)]


def attend_kernel(at_ref, row_ref, key_ref, value_ref, length_ref, out_ref, score_ref):
    new, heads = row_ref.shape[0], QH // KVH
    wide = heads * HD
    cached = key_ref.shape[1]
    step = math.gcd(cached, 512)
    member = at_ref[0] // KVH
    length = jnp.sum(
        jnp.where(iota(length_ref.shape, 1) == member, length_ref[...], 0).astype(jnp.float32),
        axis=1,
        keepdims=True,
    ).astype(jnp.int32)
    lengths = jnp.concatenate([length] * heads, axis=0)
    query = jnp.concatenate([row_ref[:, h * HD : (h + 1) * HD] for h in range(heads)], axis=0)
    rows = heads * new
    dims = (((1,), (1,)), ((), ()))
    fresh = lax.dot_general(
        query, row_ref[:, wide : wide + HD], dims, preferred_element_type=jnp.float32
    )
    causal = iota((new, new), 1) <= iota((new, new), 0)
    fresh = jnp.where(jnp.concatenate([causal] * heads, axis=0), fresh, -1e30)
    best = jnp.max(fresh, axis=1, keepdims=True)
    peak = jnp.full((rows, LANES), -1e30, jnp.float32)
    for at in range(0, cached, step):
        part = lax.dot_general(
            query, key_ref[0, at : at + step, :], dims, preferred_element_type=jnp.float32
        )
        part = jnp.where(iota((rows, step), 1) + at < lengths, part, -1e30)
        score_ref[:, at : at + step] = part
        for lane in range(0, step, LANES):
            peak = jnp.maximum(peak, part[:, lane : lane + LANES])
    best = jnp.maximum(best, jnp.max(peak, axis=1, keepdims=True))
    factor = HD ** (-0.5) * math.log2(math.e)
    fresh = jnp.exp2((fresh - best) * factor)
    sums = jnp.zeros((rows, LANES), jnp.float32)
    for at in range(0, cached, step):
        expo = jnp.exp2((score_ref[:, at : at + step] - best) * factor)
        score_ref[:, at : at + step] = expo
        for lane in range(0, step, LANES):
            sums = sums + expo[:, lane : lane + LANES]
    total = jnp.sum(fresh, axis=1, keepdims=True) + jnp.sum(sums, axis=1, keepdims=True)
    inverse = 1.0 / total
    result = jnp.dot(
        (fresh * inverse).astype(jnp.bfloat16),
        row_ref[:, wide + HD : wide + 2 * HD],
        preferred_element_type=jnp.float32,
    )
    for at in range(0, cached, step):
        result = result + jnp.dot(
            (score_ref[:, at : at + step] * inverse).astype(jnp.bfloat16),
            value_ref[0, at : at + step, :],
            preferred_element_type=jnp.float32,
        )
    result = result.astype(jnp.bfloat16)
    for h in range(heads):
        out_ref[:, h * HD : (h + 1) * HD] = result[h * new : (h + 1) * new]


def project_kernel(at_ref, even_ref, odd_ref, weight_ref, out_ref):
    me = at_ref[0]
    members, new, wide = even_ref.shape
    rows = members * new
    count = weight_ref.shape[0]
    per = count // KVH
    total = jnp.zeros((rows, LANES), jnp.float32)
    for half, ref in enumerate((even_ref, odd_ref)):
        group = (me ^ half) % KVH
        columns = jnp.concatenate(
            [weight_ref[(group * per + i) ^ me] for i in range(per)], axis=0
        )
        total = total + jnp.dot(
            ref[...].reshape(rows, wide), columns, preferred_element_type=jnp.float32
        )
    token = iota((rows, rows), 0)
    source = ((token % members) ^ (me // KVH)) * new + token // members
    pick = (iota((rows, rows), 1) == source).astype(jnp.bfloat16)
    out_ref[...] = jnp.dot(
        pick, total.astype(jnp.bfloat16), preferred_element_type=jnp.float32
    ).astype(jnp.bfloat16)


def expert_kernel(
    at_ref,
    even_ref,
    odd_ref,
    gain_ref,
    info_ref,
    gate_ref,
    up_ref,
    down_ref,
    projected_ref,
    keep_ref,
    send_ref,
    normed_ref,
):
    me = at_ref[0]
    rows = even_ref.shape[1]
    count = 2 * even_ref.shape[0]
    new = info_ref.shape[0]
    per_dev = rows // count
    members = rows // new
    experts = gate_ref.shape[0]
    width = info_ref.shape[1] // 3
    half = rows // 2

    squares = jnp.zeros((rows, LANES), jnp.float32)
    for j in range(count):
        piece = (odd_ref if j % 2 else even_ref)[j // 2].astype(jnp.float32)
        squares = squares + piece * piece
    stats = jnp.sum(squares, axis=1, keepdims=True) / (count * LANES)
    inverse = lax.rsqrt(stats + 1e-06)
    order = [2 * (b % (count // 2)) + b // (count // 2) for b in range(count)]
    own = pl.ds(pl.multiple_of(me * per_dev, per_dev), per_dev)
    for j in range(count):
        ref, i = (odd_ref if j % 2 else even_ref), j // 2
        at = pl.ds(pl.multiple_of((me ^ j) * LANES, LANES), LANES)
        gain = gain_ref[:, at].astype(jnp.float32)
        normed_ref[:, at] = (ref[i].astype(jnp.float32) * inverse * gain).astype(jnp.bfloat16)
        projected_ref[:, at] = ref[i, own, :]
    normed = jnp.concatenate(
        [
            normed_ref[pl.ds(pl.multiple_of((me ^ j) * per_dev, per_dev), per_dev), :]
            for j in order
        ],
        axis=0,
    )

    def token(shape):
        r = iota(shape, 0)
        block = (2 * ((r % half) // per_dev) + r // half) ^ me
        return block * per_dev + r % per_dev

    spread = (iota((rows, new), 1) == token((rows, new)) // members).astype(jnp.bfloat16)
    info = jnp.dot(spread, info_ref[...], preferred_element_type=jnp.float32)
    mine = iota((rows, width), 1) // TOPK == token((rows, width)) % members
    share = jnp.where(mine, info[:, width : 2 * width] + info[:, 2 * width :], 0.0)
    whole = jnp.sum(share, axis=1, keepdims=True)
    hidden = []
    for e in range(experts):
        chosen = info[:, :width] == (me * experts + e).astype(jnp.float32)
        scale = jnp.sum(jnp.where(chosen, share, 0.0), axis=1, keepdims=True) / whole
        gate = jnp.dot(normed, gate_ref[e], preferred_element_type=jnp.float32)
        up = jnp.dot(normed, up_ref[e], preferred_element_type=jnp.float32)
        hidden.append((gate / (1.0 + jnp.exp(-gate)) * up * scale).astype(jnp.bfloat16))
    step = 512
    for at in range(0, down_ref.shape[2], step):
        part = jnp.zeros((rows, step), jnp.float32)
        for e in range(experts):
            part = part + jnp.dot(
                hidden[e], down_ref[e, :, at : at + step], preferred_element_type=jnp.float32
            )
        part = part.astype(jnp.bfloat16)
        keep_ref[:, at : at + step] = part[:half]
        send_ref[:, at : at + step] = part[half:]


def swap(value, offset):
    count = lax.axis_size("seq")
    return lax.ppermute(value, "seq", [(i, i ^ offset) for i in range(count)])


def scatter_pieces(keep, send, per_dev):
    chips = keep.shape[0] // per_dev
    paired = keep + swap(send, 1)
    blocks = [paired[k * per_dev : (k + 1) * per_dev] for k in range(chips)]
    return [blocks[0]] + [swap(blocks[k], 2 * k) for k in range(1, chips)]


def gather_rows(own):
    count = lax.axis_size("seq")
    near = [own] + [swap(own, k) for k in range(4, count, 4)]
    far = [swap(piece, 2) for piece in near]
    even = jnp.stack([p for pair in zip(near, far) for p in pair], axis=0)
    return even, swap(even, 1)


def column_blocks(at, out_weight):
    count = lax.axis_size("seq")
    rows = out_weight.shape[0]
    parts = call(
        split_kernel,
        [((2, 2, rows, LANES), jnp.bfloat16)] * (count // 4),
        (at, out_weight),
        moved=4 * out_weight.size,
    )
    parts = [parts[0]] + [swap(part, 4 * k) for k, part in enumerate(parts) if k]
    near = jnp.stack([part[0] for part in parts])
    far = swap(jnp.stack([part[1] for part in parts]), 2)
    same = jnp.stack([near[:, 0], far[:, 0]], axis=1)
    other = swap(jnp.stack([near[:, 1], far[:, 1]], axis=1), 1)
    return jnp.stack([same, other], axis=2).reshape(count, rows, LANES)


def exchange_body(
    queries,
    keys,
    values,
    cache_keys,
    cache_values,
    cache_len,
    out_weight,
    norm_gain,
    expert_ids,
    route_weights,
    w_gate,
    w_up,
    w_down,
):
    count = lax.axis_size("seq")
    per_rows, members = queries.shape[0], count // KVH
    new = per_rows * count
    per_dev = per_rows * members
    rows = per_dev * count
    at = lax.axis_index("seq").astype(jnp.int32).reshape(1)
    width = -(-members * TOPK // LANES) * LANES
    wide = QH // KVH * HD
    (sent,) = call(
        pack_kernel,
        [((per_rows, count, wide + 2 * HD + 3 * width), jnp.bfloat16)],
        (queries, keys, values, expert_ids, route_weights),
    )
    taken = lax.all_to_all(sent, "seq", split_axis=1, concat_axis=0, tiled=True)
    taken = taken.reshape(new, sent.shape[2])
    columns = column_blocks(at, out_weight)
    row_count = QH // KVH * new
    (heads,) = call(
        attend_kernel,
        [((new, wide), jnp.bfloat16)],
        (at, taken, cache_keys, cache_values, cache_len),
        scratch=[pltpu.VMEM((row_count, cache_keys.shape[1]), jnp.float32)],
        flops=4 * row_count * cache_keys.shape[1] * HD,
        moved=4 * cache_keys.shape[1] * HD,
    )
    even, odd = gather_rows(heads)
    (projected,) = call(
        project_kernel,
        [((rows, LANES), jnp.bfloat16)],
        (at, even, odd, columns),
        flops=2 * rows * D * LANES,
        moved=4 * rows * D,
    )
    even, odd = gather_rows(projected)
    projected, keep, send = call(
        expert_kernel,
        [((per_dev, D), jnp.bfloat16)] + [((rows // 2, D), jnp.bfloat16)] * 2,
        (at, even, odd, norm_gain.reshape(1, D), taken[:, wide + 2 * HD :], w_gate, w_up, w_down),
        scratch=[pltpu.VMEM((rows, D), jnp.bfloat16)],
        vmem_mib=32,
        flops=6 * rows * w_gate.size,
        moved=6 * w_gate.size,
    )
    pieces = scatter_pieces(keep, send, per_dev)
    mixed = sum(piece.astype(jnp.float32) for piece in pieces)
    shape = (per_rows, members, D)
    return (projected.reshape(shape), mixed.astype(jnp.bfloat16).reshape(shape))


def fits(mesh, out_rows, positions, experts):
    count = mesh.shape["seq"]
    owned = out_rows // count
    per_dev = positions // count * (count // KVH)
    power = count & (count - 1) == 0 and count >= 8
    small = per_dev * count * D * 2 <= 2 << 20
    return power and owned == HD == LANES and count * LANES == D and per_dev % 16 == 0 and positions % 16 == 0 and small and experts <= 256


def attend(query_heads, key_rows, value_rows, lengths):
    new_count = query_heads.shape[0]
    cache_count = key_rows.shape[0] - new_count
    scores = jnp.einsum(
        "qhd,kd->hqk", query_heads, key_rows, preferred_element_type=jnp.float32
    ) * HD ** (-0.5)
    cached_ok = jnp.arange(cache_count, dtype=jnp.int32)[None, :] < lengths[:, None]
    causal_ok = (
        jnp.arange(new_count, dtype=jnp.int32)[None, :]
        <= jnp.arange(new_count, dtype=jnp.int32)[:, None]
    )
    visible = jnp.concatenate([cached_ok, causal_ok], axis=1)
    scores = jnp.where(visible[None], scores, -1e30)
    row_max = jnp.max(scores, axis=-1, keepdims=True)
    expo = jnp.exp(scores - row_max)
    row_sum = jnp.sum(expo, axis=-1, keepdims=True)
    weights = (expo / row_sum).astype(jnp.bfloat16)
    result = jnp.einsum("hqk,kd->qhd", weights, value_rows, preferred_element_type=jnp.float32)
    return result.astype(jnp.bfloat16).reshape(new_count, -1)


def plain_body(
    queries,
    keys,
    values,
    cache_keys,
    cache_values,
    cache_len,
    out_weight,
    norm_gain,
    expert_ids,
    route_weights,
    w_gate,
    w_up,
    w_down,
):
    slot_count = lax.axis_size("seq")
    per_rows = queries.shape[0]
    members = slot_count // KVH
    group_q = QH // KVH
    new_count = per_rows * slot_count
    position_index = lax.axis_index("seq")
    member = position_index // KVH
    query_rows, key_new, value_new = (
        lax.all_to_all(queries, "seq", split_axis=1, concat_axis=0, tiled=True),
        lax.all_to_all(keys, "seq", split_axis=1, concat_axis=0, tiled=True),
        lax.all_to_all(values, "seq", split_axis=1, concat_axis=0, tiled=True),
    )
    key_rows = jnp.concatenate([cache_keys[0], key_new.reshape(new_count, HD)], axis=0)
    value_rows = jnp.concatenate([cache_values[0], value_new.reshape(new_count, HD)], axis=0)
    lengths = lax.dynamic_slice_in_dim(cache_len, member, 1, 1)[:, 0]
    attended = attend(query_rows.reshape(new_count, group_q, HD), key_rows, value_rows, lengths)
    returned_heads = lax.all_to_all(
        attended[:, None, :], "seq", split_axis=0, concat_axis=1, tiled=True
    )
    token_heads = returned_heads.reshape(per_rows * members, QH * HD)
    projected_f = jnp.dot(
        token_heads,
        lax.all_gather(out_weight, "seq", axis=0, tiled=True),
        preferred_element_type=jnp.float32,
    )
    projected_f = projected_f.reshape(per_rows, members, D)
    projected = projected_f.astype(jnp.bfloat16)
    token_count = per_rows * members
    flat_rows = projected.reshape(token_count, D).astype(jnp.float32)
    stats = jnp.mean(flat_rows * flat_rows, axis=-1, keepdims=True)
    normed = (flat_rows * lax.rsqrt(stats + 1e-06) * norm_gain.astype(jnp.float32)).astype(
        jnp.bfloat16
    )
    exp_dev = w_gate.shape[0]
    expert_count = exp_dev * slot_count
    chosen_ids = expert_ids.reshape(token_count * TOPK)
    onehot = (chosen_ids[:, None] == jnp.arange(expert_count, dtype=jnp.int32)[None, :]).astype(
        jnp.int32
    )
    slot_rank = jnp.sum((jnp.cumsum(onehot, axis=0) - onehot) * onehot, axis=1)
    owner = chosen_ids // exp_dev
    local_expert = chosen_ids % exp_dev
    slot_target = (local_expert * slot_count + owner) * CAP + slot_rank
    total_slots = exp_dev * slot_count * CAP
    token_of = jnp.arange(token_count * TOPK, dtype=jnp.int32) // TOPK
    source_row = jnp.full((total_slots,), -1, jnp.int32).at[slot_target].set(token_of)
    filled = source_row >= 0
    outgoing = jnp.where(
        filled[:, None], normed[jnp.maximum(source_row, 0)], jnp.zeros((), jnp.bfloat16)
    )
    outgoing = outgoing.reshape(exp_dev, slot_count, CAP, D)
    incoming = lax.all_to_all(outgoing, "seq", split_axis=1, concat_axis=1, tiled=True)
    row_block = incoming.reshape(exp_dev, slot_count * CAP, D)
    gate_out = jnp.einsum("ecd,edf->ecf", row_block, w_gate, preferred_element_type=jnp.float32)
    up_out = jnp.einsum("ecd,edf->ecf", row_block, w_up, preferred_element_type=jnp.float32)
    hidden_act = (jax.nn.silu(gate_out) * up_out).astype(jnp.bfloat16)
    expert_out = jnp.einsum(
        "ecf,efd->ecd", hidden_act, w_down, preferred_element_type=jnp.float32
    ).astype(jnp.bfloat16)
    expert_back = lax.all_to_all(
        expert_out.reshape(exp_dev, slot_count, CAP, D),
        "seq",
        split_axis=1,
        concat_axis=1,
        tiled=True,
    )
    picked = expert_back.reshape(total_slots, D)[slot_target].reshape(token_count, TOPK, D)
    raw_weights = route_weights.reshape(token_count, TOPK)
    norm_weights = raw_weights / jnp.sum(raw_weights, axis=1, keepdims=True)
    mixed = jnp.sum(norm_weights[:, :, None] * picked.astype(jnp.float32), axis=1)
    moe_out = mixed.astype(jnp.bfloat16).reshape(per_rows, members, D)
    return (projected, moe_out)


def solution(mesh):
    def run(*args):
        chosen = exchange_body if fits(mesh, args[6].shape[0], args[0].shape[0], args[10].shape[0]) else plain_body
        return jax.shard_map(
            chosen,
            mesh=mesh,
            in_specs=(
                P("seq", "groups", None),
                P("seq", "groups", None),
                P("seq", "groups", None),
                P(("groups", "seq"), None, None),
                P(("groups", "seq"), None, None),
                P(None, "groups"),
                P("seq", None),
                P(),
                P("seq", "groups", None),
                P("seq", "groups", None),
                P("seq", None, None),
                P("seq", None, None),
                P("seq", None, None),
            ),
            out_specs=(P("seq", "groups", None), P("seq", "groups", None)),
            check_vma=False,
        )(*args)

    return run
```

```python
import functools
import math

import jax
import jax.numpy as jnp
from jax import lax
from jax.experimental import pallas as pl
from jax.experimental.pallas import tpu as pltpu
from jax.sharding import PartitionSpec as P

D = 2048
HD = 128
TOPK = 8
QH = 16
KVH = 2
CAP = 5
LANES = 128

VMEM = pl.BlockSpec(memory_space=pltpu.VMEM)
SMEM = pl.BlockSpec(memory_space=pltpu.SMEM)
ANY = pl.BlockSpec(memory_space=pl.ANY)
HBM = pl.BlockSpec(memory_space=pltpu.HBM)


def iota(shape, dim):
    return lax.broadcasted_iota(jnp.int32, shape, dim)


def call(kernel, outs, args, scratch=(), far=(), loose=(), vmem_mib=24, flops=0, moved=0):
    return pl.pallas_call(
        kernel,
        out_shape=tuple(jax.ShapeDtypeStruct(s, d) for s, d in outs),
        in_specs=[
            SMEM if a.ndim == 1 else HBM if i in far else ANY if i in loose else VMEM
            for i, a in enumerate(args)
        ],
        out_specs=tuple(VMEM for _ in outs),
        scratch_shapes=list(scratch),
        compiler_params=pltpu.CompilerParams(vmem_limit_bytes=vmem_mib << 20),
        cost_estimate=pl.CostEstimate(flops=flops, bytes_accessed=moved, transcendentals=0),
    )(*(pltpu.with_memory_space_constraint(a, pltpu.HBM) if i in far else a for i, a in enumerate(args)))


def fetch(sources, targets, sems):
    copies = [
        pltpu.make_async_copy(source, target, sems.at[i])
        for i, (source, target) in enumerate(zip(sources, targets))
    ]
    for copy in copies:
        copy.start()
    return copies


def pack_kernel(
    query_hbm,
    key_hbm,
    value_hbm,
    id_hbm,
    share_hbm,
    out_ref,
    query_ref,
    key_ref,
    value_ref,
    id_ref,
    share_ref,
    sems,
):
    refs = (id_ref, share_ref, query_ref, key_ref, value_ref)
    for copy in fetch((id_hbm, share_hbm, query_hbm, key_hbm, value_hbm), refs, sems):
        copy.wait()
    per_rows, count, wide = query_ref.shape
    members = id_ref.shape[1]
    width = (out_ref.shape[2] - wide - 2 * HD) // 3
    lane = iota((members, width), 1)
    home = lane // TOPK == iota((members, width), 0)

    def flat(table):
        total = jnp.zeros((members, width), jnp.float32)
        for k in range(TOPK):
            total = jnp.where(home & (lane % TOPK == k), table[:, k : k + 1], total)
        row = jnp.sum(total, axis=0, keepdims=True)
        return jnp.broadcast_to(row, (count, width)).astype(jnp.bfloat16)

    for i in range(per_rows):
        out_ref[i, :, :wide] = query_ref[i]
        out_ref[i, :, wide : wide + HD] = key_ref[i]
        out_ref[i, :, wide + HD : wide + 2 * HD] = value_ref[i]
        share = share_ref[i]
        high = share.astype(jnp.bfloat16).astype(jnp.float32)
        at = wide + 2 * HD
        for table in (id_ref[i].astype(jnp.float32), high, share - high):
            out_ref[i, :, at : at + width] = flat(table)
            at += width


def split_kernel(at_ref, weight_hbm, *refs):
    parts, weight_ref, sems = refs[:-2], *refs[-2:]
    fetch((weight_hbm,), (weight_ref,), sems)[0].wait()
    me = at_ref[0]
    for k, part in enumerate(parts):
        for y in range(2):
            for c in range(2):
                start = pl.multiple_of((me ^ (4 * k + 2 * y + c)) * LANES, LANES)
                part[y, c] = weight_ref[:, pl.ds(start, LANES)]


def regroup_kernel(*refs):
    parts, (_, same_ref, other_ref, send_ref) = refs[:-4], refs[-4:]
    for k, part in enumerate(parts):
        same_ref[k] = part[0, 0]
        other_ref[k] = part[0, 1]
        send_ref[0, k] = part[1, 0]
        send_ref[1, k] = part[1, 1]


def attend_kernel(
    at_ref,
    row_ref,
    length_ref,
    key_hbm,
    value_hbm,
    out_ref,
    score_ref,
    key_ref,
    value_ref,
    sems,
):
    copies = fetch((key_hbm, value_hbm), (key_ref, value_ref), sems)
    new, heads = row_ref.shape[0], QH // KVH
    wide = heads * HD
    cached = key_ref.shape[0]
    step = math.gcd(cached, 512)
    member = at_ref[0] // KVH
    length = jnp.sum(
        jnp.where(iota(length_ref.shape, 1) == member, length_ref[...], 0).astype(jnp.float32),
        axis=1,
        keepdims=True,
    ).astype(jnp.int32)
    lengths = jnp.concatenate([length] * heads, axis=0)
    query = jnp.concatenate([row_ref[:, h * HD : (h + 1) * HD] for h in range(heads)], axis=0)
    rows = heads * new
    dims = (((1,), (1,)), ((), ()))
    fresh = lax.dot_general(
        query, row_ref[:, wide : wide + HD], dims, preferred_element_type=jnp.float32
    )
    causal = iota((new, new), 1) <= iota((new, new), 0)
    fresh = jnp.where(jnp.concatenate([causal] * heads, axis=0), fresh, -1e30)
    best = jnp.max(fresh, axis=1, keepdims=True)
    peak = jnp.full((rows, LANES), -1e30, jnp.float32)
    copies[0].wait()
    for at in range(0, cached, step):
        part = lax.dot_general(
            query, key_ref[at : at + step, :], dims, preferred_element_type=jnp.float32
        )
        part = jnp.where(iota((rows, step), 1) + at < lengths, part, -1e30)
        score_ref[:, at : at + step] = part
        for lane in range(0, step, LANES):
            peak = jnp.maximum(peak, part[:, lane : lane + LANES])
    best = jnp.maximum(best, jnp.max(peak, axis=1, keepdims=True))
    factor = HD ** (-0.5) * math.log2(math.e)
    fresh = jnp.exp2((fresh - best) * factor)
    sums = jnp.zeros((rows, LANES), jnp.float32)
    for at in range(0, cached, step):
        expo = jnp.exp2((score_ref[:, at : at + step] - best) * factor)
        score_ref[:, at : at + step] = expo
        for lane in range(0, step, LANES):
            sums = sums + expo[:, lane : lane + LANES]
    total = jnp.sum(fresh, axis=1, keepdims=True) + jnp.sum(sums, axis=1, keepdims=True)
    inverse = 1.0 / total
    result = jnp.dot(
        (fresh * inverse).astype(jnp.bfloat16),
        row_ref[:, wide + HD : wide + 2 * HD],
        preferred_element_type=jnp.float32,
    )
    copies[1].wait()
    for at in range(0, cached, step):
        result = result + jnp.dot(
            (score_ref[:, at : at + step] * inverse).astype(jnp.bfloat16),
            value_ref[at : at + step, :],
            preferred_element_type=jnp.float32,
        )
    result = result.astype(jnp.bfloat16)
    for h in range(heads):
        out_ref[:, h * HD : (h + 1) * HD] = result[h * new : (h + 1) * new]


def project_kernel(at_ref, even_ref, odd_ref, *refs):
    columns_ref, (out_ref, weight_ref) = refs[:-2], refs[-2:]
    me = at_ref[0]
    members, new, wide = even_ref.shape
    rows = members * new
    count = weight_ref.shape[0]
    per = count // KVH
    for j in range(count):
        weight_ref[j] = columns_ref[j % 4][j // 4]
    total = jnp.zeros((rows, LANES), jnp.float32)
    for half, ref in enumerate((even_ref, odd_ref)):
        group = (me ^ half) % KVH
        columns = jnp.concatenate(
            [weight_ref[(group * per + i) ^ me] for i in range(per)], axis=0
        )
        total = total + jnp.dot(
            ref[...].reshape(rows, wide), columns, preferred_element_type=jnp.float32
        )
    token = iota((rows, rows), 0)
    source = ((token % members) ^ (me // KVH)) * new + token // members
    pick = (iota((rows, rows), 1) == source).astype(jnp.bfloat16)
    out_ref[...] = jnp.dot(
        pick, total.astype(jnp.bfloat16), preferred_element_type=jnp.float32
    ).astype(jnp.bfloat16)


def expert_kernel(
    at_ref,
    even_ref,
    odd_ref,
    gain_ref,
    info_ref,
    gate_ref,
    up_ref,
    down_hbm,
    projected_ref,
    keep_ref,
    send_ref,
    normed_ref,
    down_ref,
    sems,
):
    (copy,) = fetch((down_hbm,), (down_ref,), sems)
    me = at_ref[0]
    rows = even_ref.shape[1]
    count = 2 * even_ref.shape[0]
    new = info_ref.shape[0]
    per_dev = rows // count
    members = rows // new
    experts = gate_ref.shape[0]
    width = info_ref.shape[1] // 3
    half = rows // 2

    squares = jnp.zeros((rows, LANES), jnp.float32)
    for j in range(count):
        piece = (odd_ref if j % 2 else even_ref)[j // 2].astype(jnp.float32)
        squares = squares + piece * piece
    stats = jnp.sum(squares, axis=1, keepdims=True) / (count * LANES)
    inverse = lax.rsqrt(stats + 1e-06)
    order = [2 * (b % (count // 2)) + b // (count // 2) for b in range(count)]
    own = pl.ds(pl.multiple_of(me * per_dev, per_dev), per_dev)
    for j in range(count):
        ref, i = (odd_ref if j % 2 else even_ref), j // 2
        at = pl.ds(pl.multiple_of((me ^ j) * LANES, LANES), LANES)
        gain = gain_ref[:, at].astype(jnp.float32)
        normed_ref[:, at] = (ref[i].astype(jnp.float32) * inverse * gain).astype(jnp.bfloat16)
        projected_ref[:, at] = ref[i, own, :]
    normed = jnp.concatenate(
        [
            normed_ref[pl.ds(pl.multiple_of((me ^ j) * per_dev, per_dev), per_dev), :]
            for j in order
        ],
        axis=0,
    )

    def token(shape):
        r = iota(shape, 0)
        block = (2 * ((r % half) // per_dev) + r // half) ^ me
        return block * per_dev + r % per_dev

    spread = (iota((rows, new), 1) == token((rows, new)) // members).astype(jnp.bfloat16)
    info = jnp.dot(spread, info_ref[...], preferred_element_type=jnp.float32)
    mine = iota((rows, width), 1) // TOPK == token((rows, width)) % members
    share = jnp.where(mine, info[:, width : 2 * width] + info[:, 2 * width :], 0.0)
    whole = jnp.sum(share, axis=1, keepdims=True)
    hidden = []
    for e in range(experts):
        chosen = info[:, :width] == (me * experts + e).astype(jnp.float32)
        scale = jnp.sum(jnp.where(chosen, share, 0.0), axis=1, keepdims=True) / whole
        gate = jnp.dot(normed, gate_ref[e], preferred_element_type=jnp.float32)
        up = jnp.dot(normed, up_ref[e], preferred_element_type=jnp.float32)
        hidden.append((gate / (1.0 + jnp.exp(-gate)) * up * scale).astype(jnp.bfloat16))
    copy.wait()
    step = 512
    for at in range(0, down_ref.shape[2], step):
        part = jnp.zeros((rows, step), jnp.float32)
        for e in range(experts):
            part = part + jnp.dot(
                hidden[e], down_ref[e, :, at : at + step], preferred_element_type=jnp.float32
            )
        part = part.astype(jnp.bfloat16)
        keep_ref[:, at : at + step] = part[:half]
        send_ref[:, at : at + step] = part[half:]


def swap(value, offset):
    count = lax.axis_size("seq")
    return lax.ppermute(value, "seq", [(i, i ^ offset) for i in range(count)])


def scatter_pieces(keep, send, per_dev):
    chips = keep.shape[0] // per_dev
    paired = keep + swap(send, 1)
    blocks = [paired[k * per_dev : (k + 1) * per_dev] for k in range(chips)]
    return [blocks[0]] + [swap(blocks[k], 2 * k) for k in range(1, chips)]


def gather_rows(own):
    count = lax.axis_size("seq")
    near = [own] + [swap(own, k) for k in range(count - 4, 0, -4)][::-1]
    far = [swap(piece, 2) for piece in near]
    even = jnp.stack([p for pair in zip(near, far) for p in pair], axis=0)
    return even, swap(even, 1), near


def exchange_body(
    queries,
    keys,
    values,
    cache_keys,
    cache_values,
    cache_len,
    out_weight,
    norm_gain,
    expert_ids,
    route_weights,
    w_gate,
    w_up,
    w_down,
):
    count = lax.axis_size("seq")
    per_rows, members = queries.shape[0], count // KVH
    new = per_rows * count
    per_dev = per_rows * members
    rows = per_dev * count
    at = lax.axis_index("seq").astype(jnp.int32).reshape(1)
    width = -(-members * TOPK // LANES) * LANES
    wide = QH // KVH * HD
    bf16 = jnp.bfloat16
    (sent,) = call(
        pack_kernel,
        [((per_rows, count, wide + 2 * HD + 3 * width), bf16)],
        (queries, keys, values, expert_ids, route_weights),
        scratch=[
            pltpu.VMEM(a.shape, a.dtype)
            for a in (queries, keys, values, expert_ids, route_weights)
        ]
        + [pltpu.SemaphoreType.DMA((5,))],
        far=range(5),
    )
    taken = lax.all_to_all(sent, "seq", split_axis=1, concat_axis=0, tiled=True)
    taken = taken.reshape(new, sent.shape[2])
    owned = out_weight.shape[0]
    cached = cache_keys.shape[1]
    parts = call(
        split_kernel,
        [((2, 2, owned, LANES), bf16)] * (count // 4),
        (at, out_weight),
        scratch=[pltpu.VMEM(out_weight.shape, bf16), pltpu.SemaphoreType.DMA((1,))],
        far=(1,),
        moved=4 * out_weight.size,
    )
    parts = [parts[0]] + [swap(parts[k], 4 * k) for k in range(len(parts) - 1, 0, -1)][::-1]
    row_count = QH // KVH * new
    (heads,) = call(
        attend_kernel,
        [((new, wide), bf16)],
        (at, taken, cache_len, cache_keys.reshape(cached, HD), cache_values.reshape(cached, HD)),
        scratch=[
            pltpu.VMEM((row_count, cached), jnp.float32),
            pltpu.VMEM((cached, HD), bf16),
            pltpu.VMEM((cached, HD), bf16),
            pltpu.SemaphoreType.DMA((2,)),
        ],
        far=(3, 4),
        flops=4 * row_count * cached * HD,
        moved=4 * cached * HD,
    )
    even, odd, near = gather_rows(heads)
    chips = count // 4
    same, other, send = call(
        regroup_kernel,
        [((chips, owned, LANES), bf16)] * 2 + [((2, chips, owned, LANES), bf16)],
        (*parts, near[-1]),
        loose=(len(parts),),
    )
    beyond = swap(send, 2)
    columns = (same, swap(other, 1), beyond[0], swap(beyond[1], 1))
    (projected,) = call(
        project_kernel,
        [((rows, LANES), bf16)],
        (at, even, odd, *columns),
        scratch=[pltpu.VMEM((count, owned, LANES), bf16)],
        flops=2 * rows * D * LANES,
        moved=4 * rows * D,
    )
    even, odd, _ = gather_rows(projected)
    projected, keep, send = call(
        expert_kernel,
        [((per_dev, D), jnp.bfloat16)] + [((rows // 2, D), jnp.bfloat16)] * 2,
        (at, even, odd, norm_gain.reshape(1, D), taken[:, wide + 2 * HD :], w_gate, w_up, w_down),
        scratch=[
            pltpu.VMEM((rows, D), bf16),
            pltpu.VMEM(w_down.shape, bf16),
            pltpu.SemaphoreType.DMA((1,)),
        ],
        far=(7,),
        vmem_mib=32,
        flops=6 * rows * w_gate.size,
        moved=6 * w_gate.size,
    )
    pieces = scatter_pieces(keep, send, per_dev)
    mixed = sum(piece.astype(jnp.float32) for piece in pieces)
    shape = (per_rows, members, D)
    return (projected.reshape(shape), mixed.astype(jnp.bfloat16).reshape(shape))


def fits(mesh, out_rows, positions, experts):
    count = mesh.shape["seq"]
    owned = out_rows // count
    per_dev = positions // count * (count // KVH)
    power = count & (count - 1) == 0 and count >= 8
    small = per_dev * count * D * 2 <= 2 << 20
    return power and owned == HD == LANES and count * LANES == D and per_dev % 16 == 0 and positions % 16 == 0 and small and experts <= 256


def attend(query_heads, key_rows, value_rows, lengths):
    new_count = query_heads.shape[0]
    cache_count = key_rows.shape[0] - new_count
    scores = jnp.einsum(
        "qhd,kd->hqk", query_heads, key_rows, preferred_element_type=jnp.float32
    ) * HD ** (-0.5)
    cached_ok = jnp.arange(cache_count, dtype=jnp.int32)[None, :] < lengths[:, None]
    causal_ok = (
        jnp.arange(new_count, dtype=jnp.int32)[None, :]
        <= jnp.arange(new_count, dtype=jnp.int32)[:, None]
    )
    visible = jnp.concatenate([cached_ok, causal_ok], axis=1)
    scores = jnp.where(visible[None], scores, -1e30)
    row_max = jnp.max(scores, axis=-1, keepdims=True)
    expo = jnp.exp(scores - row_max)
    row_sum = jnp.sum(expo, axis=-1, keepdims=True)
    weights = (expo / row_sum).astype(jnp.bfloat16)
    result = jnp.einsum("hqk,kd->qhd", weights, value_rows, preferred_element_type=jnp.float32)
    return result.astype(jnp.bfloat16).reshape(new_count, -1)


def plain_body(
    queries,
    keys,
    values,
    cache_keys,
    cache_values,
    cache_len,
    out_weight,
    norm_gain,
    expert_ids,
    route_weights,
    w_gate,
    w_up,
    w_down,
):
    slot_count = lax.axis_size("seq")
    per_rows = queries.shape[0]
    members = slot_count // KVH
    group_q = QH // KVH
    new_count = per_rows * slot_count
    position_index = lax.axis_index("seq")
    member = position_index // KVH
    query_rows, key_new, value_new = (
        lax.all_to_all(queries, "seq", split_axis=1, concat_axis=0, tiled=True),
        lax.all_to_all(keys, "seq", split_axis=1, concat_axis=0, tiled=True),
        lax.all_to_all(values, "seq", split_axis=1, concat_axis=0, tiled=True),
    )
    key_rows = jnp.concatenate([cache_keys[0], key_new.reshape(new_count, HD)], axis=0)
    value_rows = jnp.concatenate([cache_values[0], value_new.reshape(new_count, HD)], axis=0)
    lengths = lax.dynamic_slice_in_dim(cache_len, member, 1, 1)[:, 0]
    attended = attend(query_rows.reshape(new_count, group_q, HD), key_rows, value_rows, lengths)
    returned_heads = lax.all_to_all(
        attended[:, None, :], "seq", split_axis=0, concat_axis=1, tiled=True
    )
    token_heads = returned_heads.reshape(per_rows * members, QH * HD)
    projected_f = jnp.dot(
        token_heads,
        lax.all_gather(out_weight, "seq", axis=0, tiled=True),
        preferred_element_type=jnp.float32,
    )
    projected_f = projected_f.reshape(per_rows, members, D)
    projected = projected_f.astype(jnp.bfloat16)
    token_count = per_rows * members
    flat_rows = projected.reshape(token_count, D).astype(jnp.float32)
    stats = jnp.mean(flat_rows * flat_rows, axis=-1, keepdims=True)
    normed = (flat_rows * lax.rsqrt(stats + 1e-06) * norm_gain.astype(jnp.float32)).astype(
        jnp.bfloat16
    )
    exp_dev = w_gate.shape[0]
    expert_count = exp_dev * slot_count
    chosen_ids = expert_ids.reshape(token_count * TOPK)
    onehot = (chosen_ids[:, None] == jnp.arange(expert_count, dtype=jnp.int32)[None, :]).astype(
        jnp.int32
    )
    slot_rank = jnp.sum((jnp.cumsum(onehot, axis=0) - onehot) * onehot, axis=1)
    owner = chosen_ids // exp_dev
    local_expert = chosen_ids % exp_dev
    slot_target = (local_expert * slot_count + owner) * CAP + slot_rank
    total_slots = exp_dev * slot_count * CAP
    token_of = jnp.arange(token_count * TOPK, dtype=jnp.int32) // TOPK
    source_row = jnp.full((total_slots,), -1, jnp.int32).at[slot_target].set(token_of)
    filled = source_row >= 0
    outgoing = jnp.where(
        filled[:, None], normed[jnp.maximum(source_row, 0)], jnp.zeros((), jnp.bfloat16)
    )
    outgoing = outgoing.reshape(exp_dev, slot_count, CAP, D)
    incoming = lax.all_to_all(outgoing, "seq", split_axis=1, concat_axis=1, tiled=True)
    row_block = incoming.reshape(exp_dev, slot_count * CAP, D)
    gate_out = jnp.einsum("ecd,edf->ecf", row_block, w_gate, preferred_element_type=jnp.float32)
    up_out = jnp.einsum("ecd,edf->ecf", row_block, w_up, preferred_element_type=jnp.float32)
    hidden_act = (jax.nn.silu(gate_out) * up_out).astype(jnp.bfloat16)
    expert_out = jnp.einsum(
        "ecf,efd->ecd", hidden_act, w_down, preferred_element_type=jnp.float32
    ).astype(jnp.bfloat16)
    expert_back = lax.all_to_all(
        expert_out.reshape(exp_dev, slot_count, CAP, D),
        "seq",
        split_axis=1,
        concat_axis=1,
        tiled=True,
    )
    picked = expert_back.reshape(total_slots, D)[slot_target].reshape(token_count, TOPK, D)
    raw_weights = route_weights.reshape(token_count, TOPK)
    norm_weights = raw_weights / jnp.sum(raw_weights, axis=1, keepdims=True)
    mixed = jnp.sum(norm_weights[:, :, None] * picked.astype(jnp.float32), axis=1)
    moe_out = mixed.astype(jnp.bfloat16).reshape(per_rows, members, D)
    return (projected, moe_out)


def solution(mesh):
    def run(*args):
        chosen = exchange_body if fits(mesh, args[6].shape[0], args[0].shape[0], args[10].shape[0]) else plain_body
        return jax.shard_map(
            chosen,
            mesh=mesh,
            in_specs=(
                P("seq", "groups", None),
                P("seq", "groups", None),
                P("seq", "groups", None),
                P(("groups", "seq"), None, None),
                P(("groups", "seq"), None, None),
                P(None, "groups"),
                P("seq", None),
                P(),
                P("seq", "groups", None),
                P("seq", "groups", None),
                P("seq", None, None),
                P("seq", None, None),
                P("seq", None, None),
            ),
            out_specs=(P("seq", "groups", None), P("seq", "groups", None)),
            check_vma=False,
        )(*args)

    return run
```

```python
import functools
import math

import jax
import jax.numpy as jnp
from jax import lax
from jax.experimental import pallas as pl
from jax.experimental.pallas import tpu as pltpu
from jax.sharding import PartitionSpec as P

D = 2048
HD = 128
TOPK = 8
QH = 16
KVH = 2
CAP = 5
LANES = 128

VMEM = pl.BlockSpec(memory_space=pltpu.VMEM)
SMEM = pl.BlockSpec(memory_space=pltpu.SMEM)
ANY = pl.BlockSpec(memory_space=pl.ANY)
HBM = pl.BlockSpec(memory_space=pltpu.HBM)


def iota(shape, dim):
    return lax.broadcasted_iota(jnp.int32, shape, dim)


def call(kernel, outs, args, scratch=(), far=(), loose=(), vmem_mib=12, flops=0, moved=0):
    return pl.pallas_call(
        kernel,
        out_shape=tuple(jax.ShapeDtypeStruct(s, d) for s, d in outs),
        in_specs=[
            SMEM if a.ndim == 1 else HBM if i in far else ANY if i in loose else VMEM
            for i, a in enumerate(args)
        ],
        out_specs=tuple(VMEM for _ in outs),
        scratch_shapes=list(scratch),
        compiler_params=pltpu.CompilerParams(vmem_limit_bytes=vmem_mib << 20),
        cost_estimate=pl.CostEstimate(flops=flops, bytes_accessed=moved, transcendentals=0),
    )(*(pltpu.with_memory_space_constraint(a, pltpu.HBM) if i in far else a for i, a in enumerate(args)))


def fetch(sources, targets, sems):
    copies = [
        pltpu.make_async_copy(source, target, sems.at[i])
        for i, (source, target) in enumerate(zip(sources, targets))
    ]
    for copy in copies:
        copy.start()
    return copies


def pack_kernel(
    query_hbm,
    key_hbm,
    value_hbm,
    id_hbm,
    share_hbm,
    out_ref,
    query_ref,
    key_ref,
    value_ref,
    id_ref,
    share_ref,
    sems,
):
    refs = (id_ref, share_ref, query_ref, key_ref, value_ref)
    for copy in fetch((id_hbm, share_hbm, query_hbm, key_hbm, value_hbm), refs, sems):
        copy.wait()
    per_rows, count, wide = query_ref.shape
    members = id_ref.shape[1]
    width = (out_ref.shape[2] - wide - 2 * HD) // 3
    lane = iota((members, width), 1)
    home = lane // TOPK == iota((members, width), 0)

    def flat(table):
        total = jnp.zeros((members, width), jnp.float32)
        for k in range(TOPK):
            total = jnp.where(home & (lane % TOPK == k), table[:, k : k + 1], total)
        row = jnp.sum(total, axis=0, keepdims=True)
        return jnp.broadcast_to(row, (count, width)).astype(jnp.bfloat16)

    for i in range(per_rows):
        out_ref[i, :, :wide] = query_ref[i]
        out_ref[i, :, wide : wide + HD] = key_ref[i]
        out_ref[i, :, wide + HD : wide + 2 * HD] = value_ref[i]
        share = share_ref[i]
        high = share.astype(jnp.bfloat16).astype(jnp.float32)
        at = wide + 2 * HD
        for table in (id_ref[i].astype(jnp.float32), high, share - high):
            out_ref[i, :, at : at + width] = flat(table)
            at += width


def split_kernel(at_ref, weight_hbm, *refs):
    parts, weight_ref, sems = refs[:-2], *refs[-2:]
    fetch((weight_hbm,), (weight_ref,), sems)[0].wait()
    chip = at_ref[0] // 2
    for k, part in enumerate(parts):
        for y in range(2):
            start = pl.multiple_of((chip ^ (2 * k + y)) * part.shape[2], LANES)
            part[y] = weight_ref[:, pl.ds(start, part.shape[2])]


def regroup_kernel(*refs):
    parts, (_, near_ref, far_ref) = refs[:-3], refs[-3:]
    for k, part in enumerate(parts):
        near_ref[k] = part[0]
        far_ref[k] = part[1]


def position_of(place, per_rows, core):
    return (place // per_rows * 2 + core) * per_rows + place % per_rows


def attend_kernel(
    per_rows,
    at_ref,
    row_ref,
    length_ref,
    key_hbm,
    value_hbm,
    keep_ref,
    send_ref,
    score_ref,
    key_ref,
    value_ref,
    sems,
):
    copies = fetch((key_hbm, value_hbm), (key_ref, value_ref), sems)
    new, heads = row_ref.shape[0], QH // KVH
    wide = heads * HD
    cached = key_ref.shape[0]
    step = math.gcd(cached, 512)
    member = at_ref[0] // KVH
    length = jnp.sum(
        jnp.where(iota(length_ref.shape, 1) == member, length_ref[...], 0).astype(jnp.float32),
        axis=1,
        keepdims=True,
    ).astype(jnp.int32)
    lengths = jnp.concatenate([length] * heads, axis=0)
    query = jnp.concatenate([row_ref[:, h * HD : (h + 1) * HD] for h in range(heads)], axis=0)
    rows = heads * new
    dims = (((1,), (1,)), ((), ()))
    fresh = lax.dot_general(
        query, row_ref[:, wide : wide + HD], dims, preferred_element_type=jnp.float32
    )
    causal = iota((new, new), 1) <= iota((new, new), 0)
    fresh = jnp.where(jnp.concatenate([causal] * heads, axis=0), fresh, -1e30)
    best = jnp.max(fresh, axis=1, keepdims=True)
    peak = jnp.full((rows, LANES), -1e30, jnp.float32)
    copies[0].wait()
    for at in range(0, cached, step):
        part = lax.dot_general(
            query, key_ref[at : at + step, :], dims, preferred_element_type=jnp.float32
        )
        part = jnp.where(iota((rows, step), 1) + at < lengths, part, -1e30)
        score_ref[:, at : at + step] = part
        for lane in range(0, step, LANES):
            peak = jnp.maximum(peak, part[:, lane : lane + LANES])
    best = jnp.maximum(best, jnp.max(peak, axis=1, keepdims=True))
    factor = HD ** (-0.5) * math.log2(math.e)
    fresh = jnp.exp2((fresh - best) * factor)
    sums = jnp.zeros((rows, LANES), jnp.float32)
    for at in range(0, cached, step):
        expo = jnp.exp2((score_ref[:, at : at + step] - best) * factor)
        score_ref[:, at : at + step] = expo
        for lane in range(0, step, LANES):
            sums = sums + expo[:, lane : lane + LANES]
    total = jnp.sum(fresh, axis=1, keepdims=True) + jnp.sum(sums, axis=1, keepdims=True)
    inverse = 1.0 / total
    result = jnp.dot(
        (fresh * inverse).astype(jnp.bfloat16),
        row_ref[:, wide + HD : wide + 2 * HD],
        preferred_element_type=jnp.float32,
    )
    copies[1].wait()
    for at in range(0, cached, step):
        result = result + jnp.dot(
            (score_ref[:, at : at + step] * inverse).astype(jnp.bfloat16),
            value_ref[at : at + step, :],
            preferred_element_type=jnp.float32,
        )
    result = result.astype(jnp.bfloat16)
    result = jnp.concatenate([result[h * new : (h + 1) * new] for h in range(heads)], axis=1)
    half = new // 2
    place = iota((new, new), 0)
    core = (at_ref[0] + place // half) % 2
    pick = iota((new, new), 1) == position_of(place % half, per_rows, core)
    result = jnp.dot(
        pick.astype(jnp.bfloat16), result, preferred_element_type=jnp.float32
    ).astype(jnp.bfloat16)
    keep_ref[...] = result[:half]
    send_ref[...] = result[half:]


def project_kernel(at_ref, rows_ref, *refs):
    columns, (out_ref, weight_ref) = refs[:-2], refs[-2:]
    me = at_ref[0]
    members, _, places, wide = rows_ref.shape
    rows = members * places
    owned = columns[0].shape[1]
    for i, ref in enumerate(columns):
        for k in range(ref.shape[0]):
            head = me ^ (4 * k + i)
            weight_ref[pl.ds(pl.multiple_of(head * owned, owned), owned), :] = ref[k]
    total = jnp.zeros(out_ref.shape, jnp.float32)
    for half in range(KVH):
        start = pl.multiple_of((me ^ half) % KVH * wide, wide)
        total = total + jnp.dot(
            rows_ref[:, half].reshape(rows, wide),
            weight_ref[pl.ds(start, wide), :],
            preferred_element_type=jnp.float32,
        )
    token = iota((rows, rows), 0)
    source = ((token % members) ^ (me // KVH)) * places + token // members
    pick = (iota((rows, rows), 1) == source).astype(jnp.bfloat16)
    out_ref[...] = jnp.dot(
        pick, total.astype(jnp.bfloat16), preferred_element_type=jnp.float32
    ).astype(jnp.bfloat16)


def expert_kernel(
    per_rows,
    at_ref,
    rows_ref,
    gain_ref,
    info_ref,
    gate_ref,
    up_ref,
    gate_peer_ref,
    up_peer_ref,
    down_hbm,
    down_peer_hbm,
    projected_ref,
    *refs,
):
    outs, (normed_ref, down_ref, down_peer_ref, sems) = refs[:-4], refs[-4:]
    copies = fetch((down_hbm, down_peer_hbm), (down_ref, down_peer_ref), sems)
    me = at_ref[0]
    chip, core = me // 2, me % 2
    chips, rows, lanes = rows_ref.shape
    new = info_ref.shape[0]
    per_dev = rows // chips
    members = per_dev // per_rows
    experts = gate_ref.shape[0]
    width = info_ref.shape[1] // 3

    squares = jnp.zeros((rows, lanes), jnp.float32)
    for i in range(chips):
        piece = rows_ref[i].astype(jnp.float32)
        squares = squares + piece * piece
    inverse = lax.rsqrt(jnp.sum(squares, axis=1, keepdims=True) / (chips * lanes) + 1e-06)
    own = pl.ds(pl.multiple_of(chip * per_dev, per_dev), per_dev)
    for i in range(chips):
        at = pl.ds(pl.multiple_of((chip ^ i) * lanes, lanes), lanes)
        gain = gain_ref[:, at].astype(jnp.float32)
        normed_ref[:, at] = (rows_ref[i].astype(jnp.float32) * inverse * gain).astype(jnp.bfloat16)
        projected_ref[:, at] = rows_ref[i, own, :]
    normed = jnp.concatenate(
        [
            normed_ref[pl.ds(pl.multiple_of((chip ^ i) * per_dev, per_dev), per_dev), :]
            for i in range(chips)
        ],
        axis=0,
    )

    def token(shape):
        r = iota(shape, 0)
        return ((r // per_dev) ^ chip) * per_dev + r % per_dev

    place = token((rows, new)) // members
    spread = iota((rows, new), 1) == position_of(place, per_rows, core)
    info = jnp.dot(
        spread.astype(jnp.bfloat16), info_ref[...], preferred_element_type=jnp.float32
    )
    mine = iota((rows, width), 1) // TOPK == token((rows, width)) % members
    share = jnp.where(mine, info[:, width : 2 * width] + info[:, 2 * width :], 0.0)
    whole = jnp.sum(share, axis=1, keepdims=True)
    hidden = []
    for device, gates, ups in ((me, gate_ref, up_ref), (me ^ 1, gate_peer_ref, up_peer_ref)):
        for e in range(experts):
            chosen = info[:, :width] == (device * experts + e).astype(jnp.float32)
            scale = jnp.sum(jnp.where(chosen, share, 0.0), axis=1, keepdims=True) / whole
            gate = jnp.dot(normed, gates[e], preferred_element_type=jnp.float32)
            up = jnp.dot(normed, ups[e], preferred_element_type=jnp.float32)
            hidden.append((gate / (1.0 + jnp.exp(-gate)) * up * scale).astype(jnp.bfloat16))
    for copy in copies:
        copy.wait()
    order = block_order(chips)
    step = 512
    for at in range(0, down_ref.shape[2], step):
        part = jnp.zeros((rows, step), jnp.float32)
        for e, value in enumerate(hidden):
            ref = (down_ref, down_peer_ref)[e // experts]
            part = part + jnp.dot(
                value, ref[e % experts, :, at : at + step], preferred_element_type=jnp.float32
            )
        part = part.astype(jnp.bfloat16)
        block = 0
        for out in outs:
            for i in range(out.shape[0]):
                where = order[block]
                out[i, :, at : at + step] = part[where * per_dev : (where + 1) * per_dev]
                block += 1


def block_order(chips):
    near = range(chips - 2, -1, -2)
    return [k + 1 for k in near] + list(near)


def add_kernel(near_ref, piece_ref, *outs):
    for i, out in enumerate(outs):
        out[...] = (
            near_ref[i].astype(jnp.float32) + piece_ref[i].astype(jnp.float32)
        ).astype(jnp.bfloat16)


def swap(value, offset):
    count = lax.axis_size("seq")
    return lax.ppermute(value, "seq", [(i, i ^ offset) for i in range(count)])


def scatter_pieces(far, near):
    pieces = []
    ahead = sum(part.shape[0] for part in near)
    for there, here in zip(far, near):
        shape = here.shape[1:]
        sums = call(
            add_kernel, [(shape, jnp.bfloat16)] * here.shape[0], (here, swap(there, 2))
        )
        for piece in sums:
            ahead -= 1
            pieces.append(swap(piece, 4 * ahead) if ahead else piece)
    return pieces


def gather_rows(own):
    count = lax.axis_size("seq")
    near = [own] + [swap(own, k) for k in range(count - 4, 0, -4)][::-1]
    far = [swap(piece, 2) for piece in near]
    return near, far


def interleave(near, far):
    return jnp.stack([p for pair in zip(near, far) for p in pair], axis=0)


def exchange_body(
    queries,
    keys,
    values,
    cache_keys,
    cache_values,
    cache_len,
    out_weight,
    norm_gain,
    expert_ids,
    route_weights,
    w_gate,
    w_up,
    w_down,
):
    count = lax.axis_size("seq")
    per_rows, members = queries.shape[0], count // KVH
    new = per_rows * count
    per_dev = per_rows * members
    rows = per_dev * count
    at = lax.axis_index("seq").astype(jnp.int32).reshape(1)
    width = -(-members * TOPK // LANES) * LANES
    wide = QH // KVH * HD
    bf16 = jnp.bfloat16
    (sent,) = call(
        pack_kernel,
        [((per_rows, count, wide + 2 * HD + 3 * width), bf16)],
        (queries, keys, values, expert_ids, route_weights),
        scratch=[
            pltpu.VMEM(a.shape, a.dtype)
            for a in (queries, keys, values, expert_ids, route_weights)
        ]
        + [pltpu.SemaphoreType.DMA((5,))],
        far=range(5),
    )
    taken = lax.all_to_all(sent, "seq", split_axis=1, concat_axis=0, tiled=True)
    taken = taken.reshape(new, sent.shape[2])
    owned = out_weight.shape[0]
    cached = cache_keys.shape[1]
    chips = count // 2
    lanes = D // chips
    gate_peer, up_peer, down_peer = swap(w_gate, 1), swap(w_up, 1), swap(w_down, 1)
    parts = call(
        split_kernel,
        [((2, owned, lanes), bf16)] * (chips // 2),
        (at, out_weight),
        scratch=[pltpu.VMEM(out_weight.shape, bf16), pltpu.SemaphoreType.DMA((1,))],
        far=(1,),
        moved=4 * out_weight.size,
    )
    parts = [parts[0]] + [swap(parts[k], 4 * k) for k in range(len(parts) - 1, 0, -1)][::-1]
    row_count = QH // KVH * new
    keep, send = call(
        functools.partial(attend_kernel, per_rows),
        [((new // 2, wide), bf16)] * 2,
        (at, taken, cache_len, cache_keys.reshape(cached, HD), cache_values.reshape(cached, HD)),
        scratch=[
            pltpu.VMEM((row_count, cached), jnp.float32),
            pltpu.VMEM((cached, HD), bf16),
            pltpu.VMEM((cached, HD), bf16),
            pltpu.SemaphoreType.DMA((2,)),
        ],
        far=(3, 4),
        flops=4 * row_count * cached * HD,
        moved=4 * cached * HD,
    )
    peer = swap(send, 1)
    own = jnp.stack([keep, peer])
    heads = interleave(*gather_rows(own))
    near, far = call(
        regroup_kernel,
        [((chips // 2, owned, lanes), bf16)] * 2,
        (*parts, own),
        loose=(len(parts),),
    )
    beyond = swap(far, 2)
    half = rows // 2
    (projected,) = call(
        project_kernel,
        [((half, lanes), bf16)],
        (at, heads, near, swap(near, 1), beyond, swap(beyond, 1)),
        scratch=[pltpu.VMEM((D, lanes), bf16)],
        flops=2 * half * D * lanes,
        moved=4 * half * D,
    )
    gathered = interleave(*gather_rows(projected))
    info = taken[:, wide + 2 * HD :]
    projected, *blocks = call(
        functools.partial(expert_kernel, per_rows),
        [((per_dev, D), bf16)] + [((2, per_dev, D), bf16)] * (chips // 2),
        (
            at,
            gathered,
            norm_gain.reshape(1, D),
            info,
            w_gate,
            w_up,
            gate_peer,
            up_peer,
            w_down,
            down_peer,
        ),
        scratch=[
            pltpu.VMEM((half, D), bf16),
            pltpu.VMEM(w_down.shape, bf16),
            pltpu.VMEM(w_down.shape, bf16),
            pltpu.SemaphoreType.DMA((2,)),
        ],
        far=(8, 9),
        vmem_mib=30,
        flops=12 * half * w_gate.size,
        moved=12 * w_gate.size,
    )
    pieces = scatter_pieces(blocks[: chips // 4], blocks[chips // 4 :])
    mixed = sum(piece.astype(jnp.float32) for piece in pieces)
    shape = (per_rows, members, D)
    return (projected.reshape(shape), mixed.astype(jnp.bfloat16).reshape(shape))


def fits(mesh, out_rows, positions, experts):
    count = mesh.shape["seq"]
    owned = out_rows // count
    per_dev = positions // count * (count // KVH)
    power = count & (count - 1) == 0 and count >= 8
    small = per_dev * count * D * 2 <= 2 << 20
    return power and owned == HD == LANES and count * LANES == D and per_dev % 16 == 0 and positions % 16 == 0 and small and experts <= 256


def attend(query_heads, key_rows, value_rows, lengths):
    new_count = query_heads.shape[0]
    cache_count = key_rows.shape[0] - new_count
    scores = jnp.einsum(
        "qhd,kd->hqk", query_heads, key_rows, preferred_element_type=jnp.float32
    ) * HD ** (-0.5)
    cached_ok = jnp.arange(cache_count, dtype=jnp.int32)[None, :] < lengths[:, None]
    causal_ok = (
        jnp.arange(new_count, dtype=jnp.int32)[None, :]
        <= jnp.arange(new_count, dtype=jnp.int32)[:, None]
    )
    visible = jnp.concatenate([cached_ok, causal_ok], axis=1)
    scores = jnp.where(visible[None], scores, -1e30)
    row_max = jnp.max(scores, axis=-1, keepdims=True)
    expo = jnp.exp(scores - row_max)
    row_sum = jnp.sum(expo, axis=-1, keepdims=True)
    weights = (expo / row_sum).astype(jnp.bfloat16)
    result = jnp.einsum("hqk,kd->qhd", weights, value_rows, preferred_element_type=jnp.float32)
    return result.astype(jnp.bfloat16).reshape(new_count, -1)


def plain_body(
    queries,
    keys,
    values,
    cache_keys,
    cache_values,
    cache_len,
    out_weight,
    norm_gain,
    expert_ids,
    route_weights,
    w_gate,
    w_up,
    w_down,
):
    slot_count = lax.axis_size("seq")
    per_rows = queries.shape[0]
    members = slot_count // KVH
    group_q = QH // KVH
    new_count = per_rows * slot_count
    position_index = lax.axis_index("seq")
    member = position_index // KVH
    query_rows, key_new, value_new = (
        lax.all_to_all(queries, "seq", split_axis=1, concat_axis=0, tiled=True),
        lax.all_to_all(keys, "seq", split_axis=1, concat_axis=0, tiled=True),
        lax.all_to_all(values, "seq", split_axis=1, concat_axis=0, tiled=True),
    )
    key_rows = jnp.concatenate([cache_keys[0], key_new.reshape(new_count, HD)], axis=0)
    value_rows = jnp.concatenate([cache_values[0], value_new.reshape(new_count, HD)], axis=0)
    lengths = lax.dynamic_slice_in_dim(cache_len, member, 1, 1)[:, 0]
    attended = attend(query_rows.reshape(new_count, group_q, HD), key_rows, value_rows, lengths)
    returned_heads = lax.all_to_all(
        attended[:, None, :], "seq", split_axis=0, concat_axis=1, tiled=True
    )
    token_heads = returned_heads.reshape(per_rows * members, QH * HD)
    projected_f = jnp.dot(
        token_heads,
        lax.all_gather(out_weight, "seq", axis=0, tiled=True),
        preferred_element_type=jnp.float32,
    )
    projected_f = projected_f.reshape(per_rows, members, D)
    projected = projected_f.astype(jnp.bfloat16)
    token_count = per_rows * members
    flat_rows = projected.reshape(token_count, D).astype(jnp.float32)
    stats = jnp.mean(flat_rows * flat_rows, axis=-1, keepdims=True)
    normed = (flat_rows * lax.rsqrt(stats + 1e-06) * norm_gain.astype(jnp.float32)).astype(
        jnp.bfloat16
    )
    exp_dev = w_gate.shape[0]
    expert_count = exp_dev * slot_count
    chosen_ids = expert_ids.reshape(token_count * TOPK)
    onehot = (chosen_ids[:, None] == jnp.arange(expert_count, dtype=jnp.int32)[None, :]).astype(
        jnp.int32
    )
    slot_rank = jnp.sum((jnp.cumsum(onehot, axis=0) - onehot) * onehot, axis=1)
    owner = chosen_ids // exp_dev
    local_expert = chosen_ids % exp_dev
    slot_target = (local_expert * slot_count + owner) * CAP + slot_rank
    total_slots = exp_dev * slot_count * CAP
    token_of = jnp.arange(token_count * TOPK, dtype=jnp.int32) // TOPK
    source_row = jnp.full((total_slots,), -1, jnp.int32).at[slot_target].set(token_of)
    filled = source_row >= 0
    outgoing = jnp.where(
        filled[:, None], normed[jnp.maximum(source_row, 0)], jnp.zeros((), jnp.bfloat16)
    )
    outgoing = outgoing.reshape(exp_dev, slot_count, CAP, D)
    incoming = lax.all_to_all(outgoing, "seq", split_axis=1, concat_axis=1, tiled=True)
    row_block = incoming.reshape(exp_dev, slot_count * CAP, D)
    gate_out = jnp.einsum("ecd,edf->ecf", row_block, w_gate, preferred_element_type=jnp.float32)
    up_out = jnp.einsum("ecd,edf->ecf", row_block, w_up, preferred_element_type=jnp.float32)
    hidden_act = (jax.nn.silu(gate_out) * up_out).astype(jnp.bfloat16)
    expert_out = jnp.einsum(
        "ecf,efd->ecd", hidden_act, w_down, preferred_element_type=jnp.float32
    ).astype(jnp.bfloat16)
    expert_back = lax.all_to_all(
        expert_out.reshape(exp_dev, slot_count, CAP, D),
        "seq",
        split_axis=1,
        concat_axis=1,
        tiled=True,
    )
    picked = expert_back.reshape(total_slots, D)[slot_target].reshape(token_count, TOPK, D)
    raw_weights = route_weights.reshape(token_count, TOPK)
    norm_weights = raw_weights / jnp.sum(raw_weights, axis=1, keepdims=True)
    mixed = jnp.sum(norm_weights[:, :, None] * picked.astype(jnp.float32), axis=1)
    moe_out = mixed.astype(jnp.bfloat16).reshape(per_rows, members, D)
    return (projected, moe_out)


def solution(mesh):
    def run(*args):
        exchanged = fits(mesh, args[6].shape[0], args[0].shape[0], args[10].shape[0])
        step = jax.shard_map(
            exchange_body if exchanged else plain_body,
            mesh=mesh,
            in_specs=(
                P("seq", "groups", None),
                P("seq", "groups", None),
                P("seq", "groups", None),
                P(("groups", "seq"), None, None),
                P(("groups", "seq"), None, None),
                P(None, "groups"),
                P("seq", None),
                P(),
                P("seq", "groups", None),
                P("seq", "groups", None),
                P("seq", None, None),
                P("seq", None, None),
                P("seq", None, None),
            ),
            out_specs=(P("seq", "groups", None), P("seq", "groups", None)),
            check_vma=False,
        )
        return step(*args)

    return run
```

```python
import functools
import math

import jax
import jax.numpy as jnp
from jax import lax
from jax.experimental import pallas as pl
from jax.experimental.pallas import tpu as pltpu
from jax.sharding import PartitionSpec as P

D = 2048
HD = 128
TOPK = 8
QH = 16
KVH = 2
CAP = 5
LANES = 128

VMEM = pl.BlockSpec(memory_space=pltpu.VMEM)
SMEM = pl.BlockSpec(memory_space=pltpu.SMEM)
ANY = pl.BlockSpec(memory_space=pl.ANY)
HBM = pl.BlockSpec(memory_space=pltpu.HBM)


def iota(shape, dim):
    return lax.broadcasted_iota(jnp.int32, shape, dim)


def call(kernel, outs, args, scratch=(), far=(), loose=(), vmem_mib=12, flops=0, moved=0):
    return pl.pallas_call(
        kernel,
        out_shape=tuple(jax.ShapeDtypeStruct(s, d) for s, d in outs),
        in_specs=[
            SMEM if a.ndim == 1 else HBM if i in far else ANY if i in loose else VMEM
            for i, a in enumerate(args)
        ],
        out_specs=tuple(VMEM for _ in outs),
        scratch_shapes=list(scratch),
        compiler_params=pltpu.CompilerParams(vmem_limit_bytes=vmem_mib << 20),
        cost_estimate=pl.CostEstimate(flops=flops, bytes_accessed=moved, transcendentals=0),
    )(*(pltpu.with_memory_space_constraint(a, pltpu.HBM) if i in far else a for i, a in enumerate(args)))


def fetch(sources, targets, sems):
    copies = [
        pltpu.make_async_copy(source, target, sems.at[i])
        for i, (source, target) in enumerate(zip(sources, targets))
    ]
    for copy in copies:
        copy.start()
    return copies


def pack_kernel(
    query_hbm,
    key_hbm,
    value_hbm,
    id_hbm,
    share_hbm,
    out_ref,
    query_ref,
    key_ref,
    value_ref,
    id_ref,
    share_ref,
    sems,
):
    refs = (id_ref, share_ref, query_ref, key_ref, value_ref)
    for copy in fetch((id_hbm, share_hbm, query_hbm, key_hbm, value_hbm), refs, sems):
        copy.wait()
    per_rows, count, wide = query_ref.shape
    members = id_ref.shape[1]
    width = (out_ref.shape[2] - wide - 2 * HD) // 3
    lane = iota((members, width), 1)
    home = lane // TOPK == iota((members, width), 0)

    def flat(table):
        total = jnp.zeros((members, width), jnp.float32)
        for k in range(TOPK):
            total = jnp.where(home & (lane % TOPK == k), table[:, k : k + 1], total)
        row = jnp.sum(total, axis=0, keepdims=True)
        return jnp.broadcast_to(row, (count, width)).astype(jnp.bfloat16)

    for i in range(per_rows):
        out_ref[i, :, :wide] = query_ref[i]
        out_ref[i, :, wide : wide + HD] = key_ref[i]
        out_ref[i, :, wide + HD : wide + 2 * HD] = value_ref[i]
        share = share_ref[i]
        high = share.astype(jnp.bfloat16).astype(jnp.float32)
        at = wide + 2 * HD
        for table in (id_ref[i].astype(jnp.float32), high, share - high):
            out_ref[i, :, at : at + width] = flat(table)
            at += width


def split_kernel(at_ref, weight_hbm, *refs):
    parts, sems = refs[:-1], refs[-1]
    chip = at_ref[0] // 2
    sources, targets = [], []
    for k, part in reversed(list(enumerate(parts))):
        for y in range(2):
            start = pl.multiple_of((chip ^ (2 * k + y)) * part.shape[2], LANES)
            sources.append(weight_hbm.at[:, pl.ds(start, part.shape[2])])
            targets.append(part.at[y])
    for copy in fetch(sources, targets, sems):
        copy.wait()


def regroup_kernel(*refs):
    parts, (_, near_ref, far_ref) = refs[:-3], refs[-3:]
    for k, part in enumerate(parts):
        near_ref[k] = part[0]
        far_ref[k] = part[1]


def position_of(place, per_rows, core):
    return (place // per_rows * 2 + core) * per_rows + place % per_rows


def attend_kernel(
    per_rows,
    at_ref,
    row_ref,
    length_ref,
    key_hbm,
    value_hbm,
    keep_ref,
    send_ref,
    score_ref,
    key_ref,
    value_ref,
    sems,
):
    copies = fetch((key_hbm, value_hbm), (key_ref, value_ref), sems)
    new, heads = row_ref.shape[0], QH // KVH
    wide = heads * HD
    cached = key_ref.shape[0]
    step = math.gcd(cached, 512)
    member = at_ref[0] // KVH
    length = jnp.sum(
        jnp.where(iota(length_ref.shape, 1) == member, length_ref[...], 0).astype(jnp.float32),
        axis=1,
        keepdims=True,
    ).astype(jnp.int32)
    lengths = jnp.concatenate([length] * heads, axis=0)
    query = jnp.concatenate([row_ref[:, h * HD : (h + 1) * HD] for h in range(heads)], axis=0)
    rows = heads * new
    dims = (((1,), (1,)), ((), ()))
    fresh = lax.dot_general(
        query, row_ref[:, wide : wide + HD], dims, preferred_element_type=jnp.float32
    )
    causal = iota((new, new), 1) <= iota((new, new), 0)
    fresh = jnp.where(jnp.concatenate([causal] * heads, axis=0), fresh, -1e30)
    best = jnp.max(fresh, axis=1, keepdims=True)
    peak = jnp.full((rows, LANES), -1e30, jnp.float32)
    copies[0].wait()
    for at in range(0, cached, step):
        part = lax.dot_general(
            query, key_ref[at : at + step, :], dims, preferred_element_type=jnp.float32
        )
        part = jnp.where(iota((rows, step), 1) + at < lengths, part, -1e30)
        score_ref[:, at : at + step] = part
        for lane in range(0, step, LANES):
            peak = jnp.maximum(peak, part[:, lane : lane + LANES])
    best = jnp.maximum(best, jnp.max(peak, axis=1, keepdims=True))
    factor = HD ** (-0.5) * math.log2(math.e)
    fresh = jnp.exp2((fresh - best) * factor)
    sums = jnp.zeros((rows, LANES), jnp.float32)
    for at in range(0, cached, step):
        expo = jnp.exp2((score_ref[:, at : at + step] - best) * factor)
        score_ref[:, at : at + step] = expo
        for lane in range(0, step, LANES):
            sums = sums + expo[:, lane : lane + LANES]
    total = jnp.sum(fresh, axis=1, keepdims=True) + jnp.sum(sums, axis=1, keepdims=True)
    inverse = 1.0 / total
    result = jnp.dot(
        (fresh * inverse).astype(jnp.bfloat16),
        row_ref[:, wide + HD : wide + 2 * HD],
        preferred_element_type=jnp.float32,
    )
    copies[1].wait()
    for at in range(0, cached, step):
        result = result + jnp.dot(
            (score_ref[:, at : at + step] * inverse).astype(jnp.bfloat16),
            value_ref[at : at + step, :],
            preferred_element_type=jnp.float32,
        )
    result = result.astype(jnp.bfloat16)
    result = jnp.concatenate([result[h * new : (h + 1) * new] for h in range(heads)], axis=1)
    half = new // 2
    place = iota((new, new), 0)
    core = (at_ref[0] + place // half) % 2
    pick = iota((new, new), 1) == position_of(place % half, per_rows, core)
    result = jnp.dot(
        pick.astype(jnp.bfloat16), result, preferred_element_type=jnp.float32
    ).astype(jnp.bfloat16)
    keep_ref[...] = result[:half]
    send_ref[...] = result[half:]


def project_kernel(at_ref, *refs):
    pieces, columns, (out_ref, weight_ref) = refs[:-6], refs[-6:-2], refs[-2:]
    me = at_ref[0]
    members = len(pieces)
    _, places, wide = pieces[0].shape
    rows = members * places
    owned = columns[0].shape[1]
    for i, ref in enumerate(columns):
        for k in range(ref.shape[0]):
            head = me ^ (4 * k + i)
            weight_ref[pl.ds(pl.multiple_of(head * owned, owned), owned), :] = ref[k]
    total = jnp.zeros(out_ref.shape, jnp.float32)
    for half in range(KVH):
        start = pl.multiple_of((me ^ half) % KVH * wide, wide)
        total = total + jnp.dot(
            jnp.concatenate([piece[half] for piece in pieces], axis=0),
            weight_ref[pl.ds(start, wide), :],
            preferred_element_type=jnp.float32,
        )
    token = iota((rows, rows), 0)
    source = ((token % members) ^ (me // KVH)) * places + token // members
    pick = (iota((rows, rows), 1) == source).astype(jnp.bfloat16)
    out_ref[...] = jnp.dot(
        pick, total.astype(jnp.bfloat16), preferred_element_type=jnp.float32
    ).astype(jnp.bfloat16)


def weigh(chip, odd, pieces, gain_ref, there, own_hbm, own_ref, sems):
    lanes = pieces[0].shape[1]
    experts = own_ref.shape[2]
    starts = [
        pl.multiple_of((chip ^ (2 * i + odd)) * lanes, lanes) for i in range(len(pieces))
    ]
    sources, targets = [], []
    for i, start in enumerate(starts):
        for m, source in enumerate(own_hbm):
            sources.append(source.at[:, pl.ds(start, lanes), :])
            targets.append(own_ref.at[m, i])
    copies = fetch(sources, targets, sems)
    rows = [
        (
            piece[...].astype(jnp.float32) * gain_ref[:, pl.ds(start, lanes)].astype(jnp.float32)
        ).astype(jnp.bfloat16)
        for piece, start in zip(pieces, starts)
    ]

    def products(pick):
        return [
            sum(
                jnp.dot(row, pick(m, i, e), preferred_element_type=jnp.float32)
                for i, row in enumerate(rows)
            )
            for e in range(experts)
            for m in range(2)
        ]

    out = products(lambda m, i, e: there[m][e, pl.ds(starts[i], lanes), :])
    for copy in copies:
        copy.wait()
    return out + products(lambda m, i, e: own_ref[m, i, e])


def gate_kernel(at_ref, gain_ref, gate_ref, up_ref, gate_hbm, up_hbm, *refs):
    pieces, (out_ref, own_ref, sems) = refs[:-3], refs[-3:]
    out = weigh(
        at_ref[0] // 2, 0, pieces, gain_ref, (gate_ref, up_ref), (gate_hbm, up_hbm), own_ref, sems
    )
    for i, value in enumerate(out):
        out_ref[i] = value


def block_order(chips):
    near = range(chips - 2, -1, -2)
    return [k + 1 for k in near] + list(near)


def expert_kernel(
    per_rows,
    chips,
    at_ref,
    gain_ref,
    gate_ref,
    up_ref,
    gate_hbm,
    up_hbm,
    partial_ref,
    info_ref,
    down_ref,
    down_hbm,
    *refs,
):
    near, far, projected_ref = refs[: chips // 2], refs[chips // 2 : chips], refs[chips]
    outs, (result_ref, own_ref, down_own_ref, sems, down_sems) = refs[chips + 1 : -5], refs[-5:]
    me = at_ref[0]
    chip, core = me // 2, me % 2
    rows, lanes = near[0].shape
    new = info_ref.shape[0]
    per_dev = rows // chips
    members = per_dev // per_rows
    experts = gate_ref.shape[0]
    width = info_ref.shape[1] // 3

    squares = jnp.zeros((rows, lanes), jnp.float32)
    own = pl.ds(pl.multiple_of(chip * per_dev, per_dev), per_dev)
    for i in range(chips):
        ref = (far if i % 2 else near)[i // 2]
        piece = ref[...].astype(jnp.float32)
        squares = squares + piece * piece
        projected_ref[:, pl.ds(pl.multiple_of((chip ^ i) * lanes, lanes), lanes)] = ref[own, :]
    inverse = lax.rsqrt(jnp.sum(squares, axis=1, keepdims=True) / (chips * lanes) + 1e-06)

    token = iota((rows, new), 0)
    spread = iota((rows, new), 1) == position_of(token // members, per_rows, core)
    info = jnp.dot(
        spread.astype(jnp.bfloat16), info_ref[...], preferred_element_type=jnp.float32
    )
    mine = iota((rows, width), 1) // TOPK == iota((rows, width), 0) % members
    share = jnp.where(mine, info[:, width : 2 * width] + info[:, 2 * width :], 0.0)
    whole = jnp.sum(share, axis=1, keepdims=True)

    (copy,) = fetch((down_hbm,), (down_own_ref,), down_sems)
    out = weigh(
        chip, 1, far, gain_ref, (gate_ref, up_ref), (gate_hbm, up_hbm), own_ref, sems
    )
    hidden = []
    for d in range(2 * experts):
        device = me ^ (1 - d // experts)
        chosen = info[:, :width] == (device * experts + d % experts).astype(jnp.float32)
        scale = jnp.sum(jnp.where(chosen, share, 0.0), axis=1, keepdims=True) / whole
        gate = (partial_ref[2 * d] + out[2 * d]) * inverse
        up = (partial_ref[2 * d + 1] + out[2 * d + 1]) * inverse
        hidden.append((gate / (1.0 + jnp.exp(-gate)) * up * scale).astype(jnp.bfloat16))
    copy.wait()
    step = 512
    for at in range(0, down_ref.shape[2], step):
        part = jnp.zeros((rows, step), jnp.float32)
        for d, value in enumerate(hidden):
            ref = (down_ref, down_own_ref)[d // experts]
            part = part + jnp.dot(
                value, ref[d % experts, :, at : at + step], preferred_element_type=jnp.float32
            )
        result_ref[:, at : at + step] = part.astype(jnp.bfloat16)
    order = iter(block_order(chips))
    for out in outs:
        for i in range(out.shape[0]):
            start = pl.multiple_of((chip ^ next(order)) * per_dev, per_dev)
            out[i] = result_ref[pl.ds(start, per_dev), :]


def add_kernel(near_ref, piece_ref, *outs):
    for i, out in enumerate(outs):
        out[...] = (
            near_ref[i].astype(jnp.float32) + piece_ref[i].astype(jnp.float32)
        ).astype(jnp.bfloat16)


def swap(value, offset):
    count = lax.axis_size("seq")
    return lax.ppermute(value, "seq", [(i, i ^ offset) for i in range(count)])


def scatter_pieces(far, near):
    pieces = []
    ahead = sum(part.shape[0] for part in near)
    for there, here in zip(far, near):
        shape = here.shape[1:]
        sums = call(
            add_kernel, [(shape, jnp.bfloat16)] * here.shape[0], (here, swap(there, 2))
        )
        for piece in sums:
            ahead -= 1
            pieces.append(swap(piece, 4 * ahead) if ahead else piece)
    return pieces


def gather_rows(own):
    count = lax.axis_size("seq")
    near = [own] + [swap(own, k) for k in range(count - 4, 0, -4)][::-1]
    far = [swap(piece, 2) for piece in near]
    return near, far


def exchange_body(
    queries,
    keys,
    values,
    cache_keys,
    cache_values,
    cache_len,
    out_weight,
    norm_gain,
    expert_ids,
    route_weights,
    w_gate,
    w_up,
    w_down,
):
    count = lax.axis_size("seq")
    per_rows, members = queries.shape[0], count // KVH
    new = per_rows * count
    per_dev = per_rows * members
    rows = per_dev * count
    at = lax.axis_index("seq").astype(jnp.int32).reshape(1)
    width = -(-members * TOPK // LANES) * LANES
    wide = QH // KVH * HD
    bf16 = jnp.bfloat16
    (sent,) = call(
        pack_kernel,
        [((per_rows, count, wide + 2 * HD + 3 * width), bf16)],
        (queries, keys, values, expert_ids, route_weights),
        scratch=[
            pltpu.VMEM(a.shape, a.dtype)
            for a in (queries, keys, values, expert_ids, route_weights)
        ]
        + [pltpu.SemaphoreType.DMA((5,))],
        far=range(5),
    )
    taken = lax.all_to_all(sent, "seq", split_axis=1, concat_axis=0, tiled=True)
    taken = taken.reshape(new, sent.shape[2])
    owned = out_weight.shape[0]
    cached = cache_keys.shape[1]
    chips = count // 2
    lanes = D // chips
    gate_peer, up_peer, down_peer = swap(w_gate, 1), swap(w_up, 1), swap(w_down, 1)
    parts = call(
        split_kernel,
        [((2, owned, lanes), bf16)] * (chips // 2),
        (at, out_weight),
        scratch=[pltpu.SemaphoreType.DMA((chips,))],
        far=(1,),
        moved=4 * out_weight.size,
    )
    parts = [parts[0]] + [swap(parts[k], 4 * k) for k in range(len(parts) - 1, 0, -1)][::-1]
    row_count = QH // KVH * new
    keep, send = call(
        functools.partial(attend_kernel, per_rows),
        [((new // 2, wide), bf16)] * 2,
        (at, taken, cache_len, cache_keys.reshape(cached, HD), cache_values.reshape(cached, HD)),
        scratch=[
            pltpu.VMEM((row_count, cached), jnp.float32),
            pltpu.VMEM((cached, HD), bf16),
            pltpu.VMEM((cached, HD), bf16),
            pltpu.SemaphoreType.DMA((2,)),
        ],
        far=(3, 4),
        flops=4 * row_count * cached * HD,
        moved=4 * cached * HD,
    )
    peer = swap(send, 1)
    own = jnp.stack([keep, peer])
    near, far = gather_rows(own)
    heads = [piece for pair in zip(near, far) for piece in pair]
    columns, across = call(
        regroup_kernel,
        [((chips // 2, owned, lanes), bf16)] * 2,
        (*parts, own),
        loose=(len(parts),),
    )
    beyond = swap(across, 2)
    beyond_peer = swap(beyond, 1)
    half = rows // 2
    (projected,) = call(
        project_kernel,
        [((half, lanes), bf16)],
        (at, *heads, columns, swap(columns, 1), beyond, beyond_peer),
        scratch=[pltpu.VMEM((D, lanes), bf16)],
        flops=2 * half * D * lanes,
        moved=4 * half * D,
    )
    near, far = gather_rows(projected)
    gain = norm_gain.reshape(1, D)
    experts, _, hidden = w_gate.shape
    own_rows = pltpu.VMEM((2, chips // 2, experts, lanes, hidden), bf16)
    (partial,) = call(
        gate_kernel,
        [((4 * experts, half, hidden), jnp.float32)],
        (at, gain, gate_peer, up_peer, w_gate, w_up, *near),
        scratch=[own_rows, pltpu.SemaphoreType.DMA((chips,))],
        far=(4, 5),
        vmem_mib=16,
        flops=4 * half * w_gate.size,
        moved=4 * w_gate.size,
    )
    projected, *blocks = call(
        functools.partial(expert_kernel, per_rows, chips),
        [((per_dev, D), bf16)] + [((2, per_dev, D), bf16)] * (chips // 2),
        (
            at,
            gain,
            gate_peer,
            up_peer,
            w_gate,
            w_up,
            partial,
            taken[:, wide + 2 * HD :],
            down_peer,
            w_down,
            *near,
            *far,
        ),
        scratch=[
            pltpu.VMEM((half, D), bf16),
            own_rows,
            pltpu.VMEM(w_down.shape, bf16),
            pltpu.SemaphoreType.DMA((chips,)),
            pltpu.SemaphoreType.DMA((1,)),
        ],
        far=(4, 5, 9),
        vmem_mib=24,
        flops=8 * half * w_gate.size,
        moved=8 * w_gate.size,
    )
    pieces = scatter_pieces(blocks[: chips // 4], blocks[chips // 4 :])
    mixed = sum(piece.astype(jnp.float32) for piece in pieces)
    shape = (per_rows, members, D)
    return (projected.reshape(shape), mixed.astype(jnp.bfloat16).reshape(shape))


def fits(mesh, out_rows, positions, experts):
    count = mesh.shape["seq"]
    owned = out_rows // count
    per_dev = positions // count * (count // KVH)
    power = count & (count - 1) == 0 and count >= 8
    small = per_dev * count * D * 2 <= 2 << 20
    return power and owned == HD == LANES and count * LANES == D and per_dev % 16 == 0 and positions % 16 == 0 and small and experts <= 256


def attend(query_heads, key_rows, value_rows, lengths):
    new_count = query_heads.shape[0]
    cache_count = key_rows.shape[0] - new_count
    scores = jnp.einsum(
        "qhd,kd->hqk", query_heads, key_rows, preferred_element_type=jnp.float32
    ) * HD ** (-0.5)
    cached_ok = jnp.arange(cache_count, dtype=jnp.int32)[None, :] < lengths[:, None]
    causal_ok = (
        jnp.arange(new_count, dtype=jnp.int32)[None, :]
        <= jnp.arange(new_count, dtype=jnp.int32)[:, None]
    )
    visible = jnp.concatenate([cached_ok, causal_ok], axis=1)
    scores = jnp.where(visible[None], scores, -1e30)
    row_max = jnp.max(scores, axis=-1, keepdims=True)
    expo = jnp.exp(scores - row_max)
    row_sum = jnp.sum(expo, axis=-1, keepdims=True)
    weights = (expo / row_sum).astype(jnp.bfloat16)
    result = jnp.einsum("hqk,kd->qhd", weights, value_rows, preferred_element_type=jnp.float32)
    return result.astype(jnp.bfloat16).reshape(new_count, -1)


def plain_body(
    queries,
    keys,
    values,
    cache_keys,
    cache_values,
    cache_len,
    out_weight,
    norm_gain,
    expert_ids,
    route_weights,
    w_gate,
    w_up,
    w_down,
):
    slot_count = lax.axis_size("seq")
    per_rows = queries.shape[0]
    members = slot_count // KVH
    group_q = QH // KVH
    new_count = per_rows * slot_count
    position_index = lax.axis_index("seq")
    member = position_index // KVH
    query_rows, key_new, value_new = (
        lax.all_to_all(queries, "seq", split_axis=1, concat_axis=0, tiled=True),
        lax.all_to_all(keys, "seq", split_axis=1, concat_axis=0, tiled=True),
        lax.all_to_all(values, "seq", split_axis=1, concat_axis=0, tiled=True),
    )
    key_rows = jnp.concatenate([cache_keys[0], key_new.reshape(new_count, HD)], axis=0)
    value_rows = jnp.concatenate([cache_values[0], value_new.reshape(new_count, HD)], axis=0)
    lengths = lax.dynamic_slice_in_dim(cache_len, member, 1, 1)[:, 0]
    attended = attend(query_rows.reshape(new_count, group_q, HD), key_rows, value_rows, lengths)
    returned_heads = lax.all_to_all(
        attended[:, None, :], "seq", split_axis=0, concat_axis=1, tiled=True
    )
    token_heads = returned_heads.reshape(per_rows * members, QH * HD)
    projected_f = jnp.dot(
        token_heads,
        lax.all_gather(out_weight, "seq", axis=0, tiled=True),
        preferred_element_type=jnp.float32,
    )
    projected_f = projected_f.reshape(per_rows, members, D)
    projected = projected_f.astype(jnp.bfloat16)
    token_count = per_rows * members
    flat_rows = projected.reshape(token_count, D).astype(jnp.float32)
    stats = jnp.mean(flat_rows * flat_rows, axis=-1, keepdims=True)
    normed = (flat_rows * lax.rsqrt(stats + 1e-06) * norm_gain.astype(jnp.float32)).astype(
        jnp.bfloat16
    )
    exp_dev = w_gate.shape[0]
    expert_count = exp_dev * slot_count
    chosen_ids = expert_ids.reshape(token_count * TOPK)
    onehot = (chosen_ids[:, None] == jnp.arange(expert_count, dtype=jnp.int32)[None, :]).astype(
        jnp.int32
    )
    slot_rank = jnp.sum((jnp.cumsum(onehot, axis=0) - onehot) * onehot, axis=1)
    owner = chosen_ids // exp_dev
    local_expert = chosen_ids % exp_dev
    slot_target = (local_expert * slot_count + owner) * CAP + slot_rank
    total_slots = exp_dev * slot_count * CAP
    token_of = jnp.arange(token_count * TOPK, dtype=jnp.int32) // TOPK
    source_row = jnp.full((total_slots,), -1, jnp.int32).at[slot_target].set(token_of)
    filled = source_row >= 0
    outgoing = jnp.where(
        filled[:, None], normed[jnp.maximum(source_row, 0)], jnp.zeros((), jnp.bfloat16)
    )
    outgoing = outgoing.reshape(exp_dev, slot_count, CAP, D)
    incoming = lax.all_to_all(outgoing, "seq", split_axis=1, concat_axis=1, tiled=True)
    row_block = incoming.reshape(exp_dev, slot_count * CAP, D)
    gate_out = jnp.einsum("ecd,edf->ecf", row_block, w_gate, preferred_element_type=jnp.float32)
    up_out = jnp.einsum("ecd,edf->ecf", row_block, w_up, preferred_element_type=jnp.float32)
    hidden_act = (jax.nn.silu(gate_out) * up_out).astype(jnp.bfloat16)
    expert_out = jnp.einsum(
        "ecf,efd->ecd", hidden_act, w_down, preferred_element_type=jnp.float32
    ).astype(jnp.bfloat16)
    expert_back = lax.all_to_all(
        expert_out.reshape(exp_dev, slot_count, CAP, D),
        "seq",
        split_axis=1,
        concat_axis=1,
        tiled=True,
    )
    picked = expert_back.reshape(total_slots, D)[slot_target].reshape(token_count, TOPK, D)
    raw_weights = route_weights.reshape(token_count, TOPK)
    norm_weights = raw_weights / jnp.sum(raw_weights, axis=1, keepdims=True)
    mixed = jnp.sum(norm_weights[:, :, None] * picked.astype(jnp.float32), axis=1)
    moe_out = mixed.astype(jnp.bfloat16).reshape(per_rows, members, D)
    return (projected, moe_out)


def solution(mesh):
    def run(*args):
        exchanged = fits(mesh, args[6].shape[0], args[0].shape[0], args[10].shape[0])
        step = jax.shard_map(
            exchange_body if exchanged else plain_body,
            mesh=mesh,
            in_specs=(
                P("seq", "groups", None),
                P("seq", "groups", None),
                P("seq", "groups", None),
                P(("groups", "seq"), None, None),
                P(("groups", "seq"), None, None),
                P(None, "groups"),
                P("seq", None),
                P(),
                P("seq", "groups", None),
                P("seq", "groups", None),
                P("seq", None, None),
                P("seq", None, None),
                P("seq", None, None),
            ),
            out_specs=(P("seq", "groups", None), P("seq", "groups", None)),
            check_vma=False,
        )
        return step(*args)

    return run
```

```python
import functools
import math

import jax
import jax.numpy as jnp
from jax import lax
from jax.experimental import pallas as pl
from jax.experimental.pallas import tpu as pltpu
from jax.sharding import PartitionSpec as P

D = 2048
HD = 128
TOPK = 8
QH = 16
KVH = 2
CAP = 5
LANES = 128

VMEM = pl.BlockSpec(memory_space=pltpu.VMEM)
SMEM = pl.BlockSpec(memory_space=pltpu.SMEM)
ANY = pl.BlockSpec(memory_space=pl.ANY)
HBM = pl.BlockSpec(memory_space=pltpu.HBM)


def iota(shape, dim):
    return lax.broadcasted_iota(jnp.int32, shape, dim)


def call(kernel, outs, args, scratch=(), far=(), loose=(), vmem_mib=12, flops=0, moved=0):
    return pl.pallas_call(
        kernel,
        out_shape=tuple(jax.ShapeDtypeStruct(s, d) for s, d in outs),
        in_specs=[
            SMEM if a.ndim == 1 else HBM if i in far else ANY if i in loose else VMEM
            for i, a in enumerate(args)
        ],
        out_specs=tuple(VMEM for _ in outs),
        scratch_shapes=list(scratch),
        compiler_params=pltpu.CompilerParams(vmem_limit_bytes=vmem_mib << 20),
        cost_estimate=pl.CostEstimate(flops=flops, bytes_accessed=moved, transcendentals=0),
    )(*(pltpu.with_memory_space_constraint(a, pltpu.HBM) if i in far else a for i, a in enumerate(args)))


def fetch(sources, targets, sems):
    copies = [
        pltpu.make_async_copy(source, target, sems.at[i])
        for i, (source, target) in enumerate(zip(sources, targets))
    ]
    for copy in copies:
        copy.start()
    return copies


def pack_kernel(
    query_hbm,
    key_hbm,
    value_hbm,
    id_hbm,
    share_hbm,
    length_hbm,
    at_ref,
    out_ref,
    seen_ref,
    query_ref,
    key_ref,
    value_ref,
    id_ref,
    share_ref,
    length_ref,
    sems,
):
    refs = (id_ref, share_ref, length_ref, query_ref, key_ref, value_ref)
    sources = (id_hbm, share_hbm, length_hbm, query_hbm, key_hbm, value_hbm)
    for copy in fetch(sources, refs, sems):
        copy.wait()
    new = length_ref.shape[1]
    member = at_ref[0] // KVH
    mine = jnp.where(iota(length_ref.shape, 0) == member, length_ref[...], 0).astype(jnp.float32)
    mine = jnp.broadcast_to(jnp.sum(mine, axis=0, keepdims=True), (new, new))
    mine = jnp.sum(
        jnp.where(iota((new, new), 0) == iota((new, new), 1), mine, 0.0), axis=1, keepdims=True
    )
    seen_ref[...] = jnp.broadcast_to(mine, seen_ref.shape).astype(jnp.int32)
    per_rows, count, wide = query_ref.shape
    members = id_ref.shape[1]
    width = (out_ref.shape[2] - wide - 2 * HD) // 3
    lane = iota((members, width), 1)
    home = lane // TOPK == iota((members, width), 0)

    def flat(table):
        total = jnp.zeros((members, width), jnp.float32)
        for k in range(TOPK):
            total = jnp.where(home & (lane % TOPK == k), table[:, k : k + 1], total)
        row = jnp.sum(total, axis=0, keepdims=True)
        return jnp.broadcast_to(row, (count, width)).astype(jnp.bfloat16)

    for i in range(per_rows):
        out_ref[i, :, :wide] = query_ref[i]
        out_ref[i, :, wide : wide + HD] = key_ref[i]
        out_ref[i, :, wide + HD : wide + 2 * HD] = value_ref[i]
        share = share_ref[i]
        high = share.astype(jnp.bfloat16).astype(jnp.float32)
        at = wide + 2 * HD
        for table in (id_ref[i].astype(jnp.float32), high, share - high):
            out_ref[i, :, at : at + width] = flat(table)
            at += width


def split_kernel(at_ref, group_ref, weight_hbm, *refs):
    parts, sems = refs[:-1], refs[-1]
    chip = at_ref[0] // 2
    sources, targets = [], []
    for k, part in reversed(list(enumerate(parts))):
        for y in range(2):
            start = pl.multiple_of((chip ^ (2 * k + y)) * part.shape[2], LANES)
            rows = pl.ds(pl.multiple_of(group_ref[0] * part.shape[1], 16), part.shape[1])
            sources.append(weight_hbm.at[rows, pl.ds(start, part.shape[2])])
            targets.append(part.at[y])
    for copy in fetch(sources, targets, sems):
        copy.wait()


def regroup_kernel(*refs):
    parts, (_, near_ref, far_ref) = refs[:-3], refs[-3:]
    for k, part in enumerate(parts):
        near_ref[k] = part[0]
        far_ref[k] = part[1]


def position_of(place, per_rows, core):
    return (place // per_rows * 2 + core) * per_rows + place % per_rows


def attend_kernel(
    per_rows,
    at_ref,
    row_ref,
    length_ref,
    key_hbm,
    value_hbm,
    keep_ref,
    send_ref,
    score_ref,
    key_ref,
    value_ref,
    sems,
):
    copies = fetch((key_hbm, value_hbm), (key_ref, value_ref), sems)
    new, heads = row_ref.shape[0], QH // KVH
    wide = heads * HD
    cached = key_ref.shape[0]
    step = math.gcd(cached, 512)
    length = length_ref[:, :1]
    lengths = jnp.concatenate([length] * heads, axis=0)
    query = jnp.concatenate([row_ref[:, h * HD : (h + 1) * HD] for h in range(heads)], axis=0)
    rows = heads * new
    dims = (((1,), (1,)), ((), ()))
    fresh = lax.dot_general(
        query, row_ref[:, wide : wide + HD], dims, preferred_element_type=jnp.float32
    )
    causal = iota((new, new), 1) <= iota((new, new), 0)
    fresh = jnp.where(jnp.concatenate([causal] * heads, axis=0), fresh, -1e30)
    best = jnp.max(fresh, axis=1, keepdims=True)
    peak = jnp.full((rows, LANES), -1e30, jnp.float32)
    copies[0].wait()
    for at in range(0, cached, step):
        part = lax.dot_general(
            query, key_ref[at : at + step, :], dims, preferred_element_type=jnp.float32
        )
        part = jnp.where(iota((rows, step), 1) + at < lengths, part, -1e30)
        score_ref[:, at : at + step] = part
        for lane in range(0, step, LANES):
            peak = jnp.maximum(peak, part[:, lane : lane + LANES])
    best = jnp.maximum(best, jnp.max(peak, axis=1, keepdims=True))
    factor = HD ** (-0.5) * math.log2(math.e)
    fresh = jnp.exp2((fresh - best) * factor)
    sums = jnp.zeros((rows, LANES), jnp.float32)
    for at in range(0, cached, step):
        expo = jnp.exp2((score_ref[:, at : at + step] - best) * factor)
        score_ref[:, at : at + step] = expo
        for lane in range(0, step, LANES):
            sums = sums + expo[:, lane : lane + LANES]
    total = jnp.sum(fresh, axis=1, keepdims=True) + jnp.sum(sums, axis=1, keepdims=True)
    inverse = 1.0 / total
    result = jnp.dot(
        (fresh * inverse).astype(jnp.bfloat16),
        row_ref[:, wide + HD : wide + 2 * HD],
        preferred_element_type=jnp.float32,
    )
    copies[1].wait()
    for at in range(0, cached, step):
        result = result + jnp.dot(
            (score_ref[:, at : at + step] * inverse).astype(jnp.bfloat16),
            value_ref[at : at + step, :],
            preferred_element_type=jnp.float32,
        )
    result = result.astype(jnp.bfloat16)
    result = jnp.concatenate([result[h * new : (h + 1) * new] for h in range(heads)], axis=1)
    half = new // 2
    place = iota((new, new), 0)
    core = (at_ref[0] + place // half) % 2
    pick = iota((new, new), 1) == position_of(place % half, per_rows, core)
    result = jnp.dot(
        pick.astype(jnp.bfloat16), result, preferred_element_type=jnp.float32
    ).astype(jnp.bfloat16)
    keep_ref[...] = result[:half]
    send_ref[...] = result[half:]


def project_kernel(at_ref, group_ref, *refs):
    pieces, columns, (out_ref, weight_ref) = refs[:-10], refs[-10:-2], refs[-2:]
    me = at_ref[0]
    members = len(pieces)
    _, places, wide = pieces[0].shape
    rows = members * places
    part = columns[0].shape[1]
    for i, ref in enumerate(columns):
        for k in range(ref.shape[0]):
            place = 2 * (me ^ (4 * k + i // 2)) + (group_ref[0] ^ (i % 2))
            weight_ref[pl.ds(pl.multiple_of(place * part, part), part), :] = ref[k]
    total = jnp.zeros(out_ref.shape, jnp.float32)
    for half in range(KVH):
        start = pl.multiple_of((me ^ half) % KVH * wide, wide)
        total = total + jnp.dot(
            jnp.concatenate([piece[half] for piece in pieces], axis=0),
            weight_ref[pl.ds(start, wide), :],
            preferred_element_type=jnp.float32,
        )
    token = iota((rows, rows), 0)
    source = ((token % members) ^ (me // KVH)) * places + token // members
    pick = (iota((rows, rows), 1) == source).astype(jnp.bfloat16)
    out_ref[...] = jnp.dot(
        pick, total.astype(jnp.bfloat16), preferred_element_type=jnp.float32
    ).astype(jnp.bfloat16)


def weigh(chip, odd, pieces, gain_ref, there, own_hbm, own_ref, sems):
    lanes = pieces[0].shape[1]
    experts = own_ref.shape[1]
    starts = [
        pl.multiple_of((chip ^ (2 * i + odd)) * lanes, lanes) for i in range(len(pieces))
    ]
    sources, targets = [], []
    for i, start in enumerate(starts):
        for m, source in enumerate(own_hbm):
            sources.append(source.at[:, pl.ds(start, lanes), :])
            targets.append(own_ref.at[m, :, pl.ds(i * lanes, lanes), :])
    copies = fetch(sources, targets, sems)
    rows = jnp.concatenate(
        [
            (
                piece[...].astype(jnp.float32)
                * gain_ref[:, pl.ds(start, lanes)].astype(jnp.float32)
            ).astype(jnp.bfloat16)
            for piece, start in zip(pieces, starts)
        ],
        axis=1,
    )

    def products(pick):
        return [
            jnp.dot(
                rows,
                jnp.concatenate([pick(0, e), pick(1, e)], axis=1),
                preferred_element_type=jnp.float32,
            )
            for e in range(experts)
        ]

    out = products(
        lambda m, e: jnp.concatenate(
            [there[m][e, pl.ds(start, lanes), :] for start in starts], axis=0
        )
    )
    for copy in copies:
        copy.wait()
    return out + products(lambda m, e: own_ref[m, e])


def gate_kernel(at_ref, gain_ref, gate_ref, up_ref, gate_hbm, up_hbm, *refs):
    pieces, (out_ref, own_ref, sems) = refs[:-3], refs[-3:]
    out = weigh(
        at_ref[0] // 2, 0, pieces, gain_ref, (gate_ref, up_ref), (gate_hbm, up_hbm), own_ref, sems
    )
    for i, value in enumerate(out):
        out_ref[i] = value


def block_order(chips):
    near = range(chips - 2, -1, -2)
    return [k + 1 for k in near] + list(near)


def expert_kernel(
    per_rows,
    chips,
    at_ref,
    gain_ref,
    gate_ref,
    up_ref,
    gate_hbm,
    up_hbm,
    partial_ref,
    info_ref,
    down_ref,
    down_hbm,
    *refs,
):
    near, far, projected_ref = refs[: chips // 2], refs[chips // 2 : chips], refs[chips]
    outs, (result_ref, own_ref, sems) = refs[chips + 1 : -3], refs[-3:]
    me = at_ref[0]
    chip, core = me // 2, me % 2
    rows, lanes = near[0].shape
    new = info_ref.shape[0]
    per_dev = rows // chips
    members = per_dev // per_rows
    experts = gate_ref.shape[0]
    width = info_ref.shape[1] // 3

    squares = jnp.zeros((rows, lanes), jnp.float32)
    own = pl.ds(pl.multiple_of(chip * per_dev, per_dev), per_dev)
    for i in range(chips):
        ref = (far if i % 2 else near)[i // 2]
        piece = ref[...].astype(jnp.float32)
        squares = squares + piece * piece
        projected_ref[:, pl.ds(pl.multiple_of((chip ^ i) * lanes, lanes), lanes)] = ref[own, :]
    inverse = lax.rsqrt(jnp.sum(squares, axis=1, keepdims=True) / (chips * lanes) + 1e-06)

    token = iota((rows, new), 0)
    spread = iota((rows, new), 1) == position_of(token // members, per_rows, core)
    info = jnp.dot(
        spread.astype(jnp.bfloat16), info_ref[...], preferred_element_type=jnp.float32
    )
    mine = iota((rows, width), 1) // TOPK == iota((rows, width), 0) % members
    share = jnp.where(mine, info[:, width : 2 * width] + info[:, 2 * width :], 0.0)
    whole = jnp.sum(share, axis=1, keepdims=True)

    out = weigh(
        chip, 1, far, gain_ref, (gate_ref, up_ref), (gate_hbm, up_hbm), own_ref, sems
    )
    hidden = []
    for d in range(2 * experts):
        device = me ^ (1 - d // experts)
        chosen = info[:, :width] == (device * experts + d % experts).astype(jnp.float32)
        scale = jnp.sum(jnp.where(chosen, share, 0.0), axis=1, keepdims=True) / whole
        both = (partial_ref[d] + out[d]) * inverse
        gate, up = both[:, : both.shape[1] // 2], both[:, both.shape[1] // 2 :]
        hidden.append((gate / (1.0 + jnp.exp(-gate)) * up * scale).astype(jnp.bfloat16))
    step = 512
    for at in range(0, down_ref.shape[2], step):
        part = jnp.zeros((rows, step), jnp.float32)
        for d, ref in enumerate((down_ref, down_hbm)):
            part = part + jnp.dot(
                jnp.concatenate(hidden[d * experts : (d + 1) * experts], axis=1),
                ref[:, :, at : at + step].reshape(-1, step),
                preferred_element_type=jnp.float32,
            )
        result_ref[:, at : at + step] = part.astype(jnp.bfloat16)
    order = iter(block_order(chips))
    for out in outs:
        for i in range(out.shape[0]):
            start = pl.multiple_of((chip ^ next(order)) * per_dev, per_dev)
            out[i] = result_ref[pl.ds(start, per_dev), :]


def add_kernel(near_ref, piece_ref, *outs):
    for i, out in enumerate(outs):
        out[...] = (
            near_ref[i].astype(jnp.float32) + piece_ref[i].astype(jnp.float32)
        ).astype(jnp.bfloat16)


def sum_kernel(*refs):
    total = refs[0][...].astype(jnp.float32)
    for ref in refs[1:-1]:
        total = total + ref[...].astype(jnp.float32)
    refs[-1][...] = total.astype(jnp.bfloat16)


def swap(value, offset):
    count = lax.axis_size("seq")
    return lax.ppermute(value, "seq", [(i, i ^ offset) for i in range(count)])


def cross(value):
    return lax.ppermute(value, "groups", [(0, 1), (1, 0)])


def scatter_pieces(far, near):
    pieces = []
    ahead = sum(part.shape[0] for part in near)
    for there, here in zip(far, near):
        shape = here.shape[1:]
        sums = call(
            add_kernel, [(shape, jnp.bfloat16)] * here.shape[0], (here, swap(there, 2))
        )
        for piece in sums:
            ahead -= 1
            pieces.append(swap(piece, 4 * ahead) if ahead else piece)
    return pieces


def gather_rows(own):
    count = lax.axis_size("seq")
    near = [own] + [swap(own, k) for k in range(count - 4, 0, -4)][::-1]
    far = [swap(piece, 2) for piece in near]
    return near, far


def exchange_body(
    queries,
    keys,
    values,
    cache_keys,
    cache_values,
    cache_len,
    out_weight,
    norm_gain,
    expert_ids,
    route_weights,
    w_gate,
    w_up,
    w_down,
):
    count = lax.axis_size("seq")
    per_rows, members = queries.shape[0], count // KVH
    new = per_rows * count
    per_dev = per_rows * members
    rows = per_dev * count
    at = lax.axis_index("seq").astype(jnp.int32).reshape(1)
    group = lax.axis_index("groups").astype(jnp.int32).reshape(1)
    width = -(-members * TOPK // LANES) * LANES
    wide = QH // KVH * HD
    bf16 = jnp.bfloat16
    loads = (queries, keys, values, expert_ids, route_weights, cache_len.T)
    sent, seen = call(
        pack_kernel,
        [
            ((per_rows, count, wide + 2 * HD + 3 * width), bf16),
            ((new, LANES), jnp.int32),
        ],
        (*loads, at),
        scratch=[pltpu.VMEM(a.shape, a.dtype) for a in loads] + [pltpu.SemaphoreType.DMA((6,))],
        far=range(6),
    )
    taken = lax.all_to_all(sent, "seq", split_axis=1, concat_axis=0, tiled=True)
    taken = taken.reshape(new, sent.shape[2])
    owned = out_weight.shape[0]
    cached = cache_keys.shape[1]
    chips = count // 2
    lanes = D // chips
    gate_peer, up_peer, down_peer = swap(w_gate, 1), swap(w_up, 1), swap(w_down, 1)
    parts = call(
        split_kernel,
        [((2, owned // 2, lanes), bf16)] * (chips // 2),
        (at, group, out_weight),
        scratch=[pltpu.SemaphoreType.DMA((chips,))],
        far=(2,),
        moved=4 * out_weight.size,
    )
    parts = [parts[0]] + [swap(parts[k], 4 * k) for k in range(len(parts) - 1, 0, -1)][::-1]
    row_count = QH // KVH * new
    keep, send = call(
        functools.partial(attend_kernel, per_rows),
        [((new // 2, wide), bf16)] * 2,
        (at, taken, seen, cache_keys.reshape(cached, HD), cache_values.reshape(cached, HD)),
        scratch=[
            pltpu.VMEM((row_count, cached), jnp.float32),
            pltpu.VMEM((cached, HD), bf16),
            pltpu.VMEM((cached, HD), bf16),
            pltpu.SemaphoreType.DMA((2,)),
        ],
        far=(3, 4),
        flops=4 * row_count * cached * HD,
        moved=4 * cached * HD,
    )
    peer = swap(send, 1)
    own = jnp.stack([keep, peer])
    near, far = gather_rows(own)
    heads = [piece for pair in zip(near, far) for piece in pair]
    columns, across = call(
        regroup_kernel,
        [((chips // 2, owned // 2, lanes), bf16)] * 2,
        (*parts, own),
        loose=(len(parts),),
    )
    beyond = swap(across, 2)
    columns_there = cross(columns)
    beyond_there = cross(beyond)
    blocks = [columns, columns_there]
    blocks += [swap(block, 1) for block in blocks]
    blocks += [beyond, beyond_there]
    blocks += [swap(block, 1) for block in blocks[-2:]]
    half = rows // 2
    (projected,) = call(
        project_kernel,
        [((half, lanes), bf16)],
        (at, group, *heads, *blocks),
        scratch=[pltpu.VMEM((D, lanes), bf16)],
        flops=2 * half * D * lanes,
        moved=4 * half * D,
    )
    near, far = gather_rows(projected)
    gain = norm_gain.reshape(1, D)
    experts, _, hidden = w_gate.shape
    own_rows = pltpu.VMEM((2, experts, D // 2, hidden), bf16)
    (partial,) = call(
        gate_kernel,
        [((2 * experts, half, 2 * hidden), jnp.float32)],
        (at, gain, gate_peer, up_peer, w_gate, w_up, *near),
        scratch=[own_rows, pltpu.SemaphoreType.DMA((chips,))],
        far=(4, 5),
        vmem_mib=16,
        flops=4 * half * w_gate.size,
        moved=4 * w_gate.size,
    )
    projected, *blocks = call(
        functools.partial(expert_kernel, per_rows, chips),
        [((per_dev, D), bf16)] + [((2, per_dev, D), bf16)] * (chips // 2),
        (
            at,
            gain,
            gate_peer,
            up_peer,
            w_gate,
            w_up,
            partial,
            taken[:, wide + 2 * HD :],
            down_peer,
            w_down,
            *near,
            *far,
        ),
        scratch=[
            pltpu.VMEM((half, D), bf16),
            own_rows,
            pltpu.SemaphoreType.DMA((chips,)),
        ],
        far=(4, 5),
        vmem_mib=24,
        flops=8 * half * w_gate.size,
        moved=8 * w_gate.size,
    )
    pieces = scatter_pieces(blocks[: chips // 4], blocks[chips // 4 :])
    (mixed,) = call(sum_kernel, [((per_dev, D), bf16)], pieces)
    shape = (per_rows, members, D)
    return (projected.reshape(shape), mixed.reshape(shape))


def fits(mesh, out_rows, positions, experts):
    count = mesh.shape["seq"]
    owned = out_rows // count
    per_dev = positions // count * (count // KVH)
    pair = mesh.shape["groups"] == 2
    power = count & (count - 1) == 0 and count >= 8
    small = per_dev * count * D * 2 <= 2 << 20
    return pair and power and owned == HD == LANES and count * LANES == D and per_dev % 16 == 0 and positions % 16 == 0 and small and experts <= 256


def attend(query_heads, key_rows, value_rows, lengths):
    new_count = query_heads.shape[0]
    cache_count = key_rows.shape[0] - new_count
    scores = jnp.einsum(
        "qhd,kd->hqk", query_heads, key_rows, preferred_element_type=jnp.float32
    ) * HD ** (-0.5)
    cached_ok = jnp.arange(cache_count, dtype=jnp.int32)[None, :] < lengths[:, None]
    causal_ok = (
        jnp.arange(new_count, dtype=jnp.int32)[None, :]
        <= jnp.arange(new_count, dtype=jnp.int32)[:, None]
    )
    visible = jnp.concatenate([cached_ok, causal_ok], axis=1)
    scores = jnp.where(visible[None], scores, -1e30)
    row_max = jnp.max(scores, axis=-1, keepdims=True)
    expo = jnp.exp(scores - row_max)
    row_sum = jnp.sum(expo, axis=-1, keepdims=True)
    weights = (expo / row_sum).astype(jnp.bfloat16)
    result = jnp.einsum("hqk,kd->qhd", weights, value_rows, preferred_element_type=jnp.float32)
    return result.astype(jnp.bfloat16).reshape(new_count, -1)


def plain_body(
    queries,
    keys,
    values,
    cache_keys,
    cache_values,
    cache_len,
    out_weight,
    norm_gain,
    expert_ids,
    route_weights,
    w_gate,
    w_up,
    w_down,
):
    slot_count = lax.axis_size("seq")
    per_rows = queries.shape[0]
    members = slot_count // KVH
    group_q = QH // KVH
    new_count = per_rows * slot_count
    position_index = lax.axis_index("seq")
    member = position_index // KVH
    query_rows, key_new, value_new = (
        lax.all_to_all(queries, "seq", split_axis=1, concat_axis=0, tiled=True),
        lax.all_to_all(keys, "seq", split_axis=1, concat_axis=0, tiled=True),
        lax.all_to_all(values, "seq", split_axis=1, concat_axis=0, tiled=True),
    )
    key_rows = jnp.concatenate([cache_keys[0], key_new.reshape(new_count, HD)], axis=0)
    value_rows = jnp.concatenate([cache_values[0], value_new.reshape(new_count, HD)], axis=0)
    lengths = lax.dynamic_slice_in_dim(cache_len, member, 1, 1)[:, 0]
    attended = attend(query_rows.reshape(new_count, group_q, HD), key_rows, value_rows, lengths)
    returned_heads = lax.all_to_all(
        attended[:, None, :], "seq", split_axis=0, concat_axis=1, tiled=True
    )
    token_heads = returned_heads.reshape(per_rows * members, QH * HD)
    projected_f = jnp.dot(
        token_heads,
        lax.all_gather(out_weight, "seq", axis=0, tiled=True),
        preferred_element_type=jnp.float32,
    )
    projected_f = projected_f.reshape(per_rows, members, D)
    projected = projected_f.astype(jnp.bfloat16)
    token_count = per_rows * members
    flat_rows = projected.reshape(token_count, D).astype(jnp.float32)
    stats = jnp.mean(flat_rows * flat_rows, axis=-1, keepdims=True)
    normed = (flat_rows * lax.rsqrt(stats + 1e-06) * norm_gain.astype(jnp.float32)).astype(
        jnp.bfloat16
    )
    exp_dev = w_gate.shape[0]
    expert_count = exp_dev * slot_count
    chosen_ids = expert_ids.reshape(token_count * TOPK)
    onehot = (chosen_ids[:, None] == jnp.arange(expert_count, dtype=jnp.int32)[None, :]).astype(
        jnp.int32
    )
    slot_rank = jnp.sum((jnp.cumsum(onehot, axis=0) - onehot) * onehot, axis=1)
    owner = chosen_ids // exp_dev
    local_expert = chosen_ids % exp_dev
    slot_target = (local_expert * slot_count + owner) * CAP + slot_rank
    total_slots = exp_dev * slot_count * CAP
    token_of = jnp.arange(token_count * TOPK, dtype=jnp.int32) // TOPK
    source_row = jnp.full((total_slots,), -1, jnp.int32).at[slot_target].set(token_of)
    filled = source_row >= 0
    outgoing = jnp.where(
        filled[:, None], normed[jnp.maximum(source_row, 0)], jnp.zeros((), jnp.bfloat16)
    )
    outgoing = outgoing.reshape(exp_dev, slot_count, CAP, D)
    incoming = lax.all_to_all(outgoing, "seq", split_axis=1, concat_axis=1, tiled=True)
    row_block = incoming.reshape(exp_dev, slot_count * CAP, D)
    gate_out = jnp.einsum("ecd,edf->ecf", row_block, w_gate, preferred_element_type=jnp.float32)
    up_out = jnp.einsum("ecd,edf->ecf", row_block, w_up, preferred_element_type=jnp.float32)
    hidden_act = (jax.nn.silu(gate_out) * up_out).astype(jnp.bfloat16)
    expert_out = jnp.einsum(
        "ecf,efd->ecd", hidden_act, w_down, preferred_element_type=jnp.float32
    ).astype(jnp.bfloat16)
    expert_back = lax.all_to_all(
        expert_out.reshape(exp_dev, slot_count, CAP, D),
        "seq",
        split_axis=1,
        concat_axis=1,
        tiled=True,
    )
    picked = expert_back.reshape(total_slots, D)[slot_target].reshape(token_count, TOPK, D)
    raw_weights = route_weights.reshape(token_count, TOPK)
    norm_weights = raw_weights / jnp.sum(raw_weights, axis=1, keepdims=True)
    mixed = jnp.sum(norm_weights[:, :, None] * picked.astype(jnp.float32), axis=1)
    moe_out = mixed.astype(jnp.bfloat16).reshape(per_rows, members, D)
    return (projected, moe_out)


def solution(mesh):
    def run(*args):
        exchanged = fits(mesh, args[6].shape[0], args[0].shape[0], args[10].shape[0])
        step = jax.shard_map(
            exchange_body if exchanged else plain_body,
            mesh=mesh,
            in_specs=(
                P("seq", "groups", None),
                P("seq", "groups", None),
                P("seq", "groups", None),
                P(("groups", "seq"), None, None),
                P(("groups", "seq"), None, None),
                P(None, "groups"),
                P("seq", None),
                P(),
                P("seq", "groups", None),
                P("seq", "groups", None),
                P("seq", None, None),
                P("seq", None, None),
                P("seq", None, None),
            ),
            out_specs=(P("seq", "groups", None), P("seq", "groups", None)),
            check_vma=False,
        )
        return step(*args)

    return run
```

```python
import functools
import math

import jax
import jax.numpy as jnp
from jax import lax
from jax.experimental import pallas as pl
from jax.experimental.pallas import tpu as pltpu
from jax.sharding import PartitionSpec as P

D = 2048
HD = 128
TOPK = 8
QH = 16
KVH = 2
CAP = 5
LANES = 128

VMEM = pl.BlockSpec(memory_space=pltpu.VMEM)
SMEM = pl.BlockSpec(memory_space=pltpu.SMEM)
ANY = pl.BlockSpec(memory_space=pl.ANY)
HBM = pl.BlockSpec(memory_space=pltpu.HBM)


def iota(shape, dim):
    return lax.broadcasted_iota(jnp.int32, shape, dim)


def call(kernel, outs, args, scratch=(), far=(), loose=(), vmem_mib=12, flops=0, moved=0):
    return pl.pallas_call(
        kernel,
        out_shape=tuple(jax.ShapeDtypeStruct(s, d) for s, d in outs),
        in_specs=[
            SMEM if a.ndim == 1 else HBM if i in far else ANY if i in loose else VMEM
            for i, a in enumerate(args)
        ],
        out_specs=tuple(VMEM for _ in outs),
        scratch_shapes=list(scratch),
        compiler_params=pltpu.CompilerParams(vmem_limit_bytes=vmem_mib << 20),
        cost_estimate=pl.CostEstimate(flops=flops, bytes_accessed=moved, transcendentals=0),
    )(*(pltpu.with_memory_space_constraint(a, pltpu.HBM) if i in far else a for i, a in enumerate(args)))


def fetch(sources, targets, sems):
    copies = [
        pltpu.make_async_copy(source, target, sems.at[i])
        for i, (source, target) in enumerate(zip(sources, targets))
    ]
    for copy in copies:
        copy.start()
    return copies


def pack_kernel(
    query_hbm,
    key_hbm,
    value_hbm,
    id_hbm,
    share_hbm,
    length_hbm,
    at_ref,
    out_ref,
    seen_ref,
    query_ref,
    key_ref,
    value_ref,
    id_ref,
    share_ref,
    length_ref,
    sems,
):
    refs = (id_ref, share_ref, length_ref, query_ref, key_ref, value_ref)
    sources = (id_hbm, share_hbm, length_hbm, query_hbm, key_hbm, value_hbm)
    for copy in fetch(sources, refs, sems):
        copy.wait()
    new = length_ref.shape[1]
    member = at_ref[0] // KVH
    mine = jnp.where(iota(length_ref.shape, 0) == member, length_ref[...], 0).astype(jnp.float32)
    mine = jnp.broadcast_to(jnp.sum(mine, axis=0, keepdims=True), (new, new))
    mine = jnp.sum(
        jnp.where(iota((new, new), 0) == iota((new, new), 1), mine, 0.0), axis=1, keepdims=True
    )
    seen_ref[...] = jnp.broadcast_to(mine, seen_ref.shape).astype(jnp.int32)
    per_rows, count, wide = query_ref.shape
    members = id_ref.shape[1]
    width = (out_ref.shape[2] - wide - 2 * HD) // 3
    lane = iota((members, width), 1)
    home = lane // TOPK == iota((members, width), 0)

    def flat(table):
        total = jnp.zeros((members, width), jnp.float32)
        for k in range(TOPK):
            total = jnp.where(home & (lane % TOPK == k), table[:, k : k + 1], total)
        row = jnp.sum(total, axis=0, keepdims=True)
        return jnp.broadcast_to(row, (count, width)).astype(jnp.bfloat16)

    for i in range(per_rows):
        out_ref[i, :, :wide] = query_ref[i]
        out_ref[i, :, wide : wide + HD] = key_ref[i]
        out_ref[i, :, wide + HD : wide + 2 * HD] = value_ref[i]
        share = share_ref[i]
        high = share.astype(jnp.bfloat16).astype(jnp.float32)
        at = wide + 2 * HD
        for table in (id_ref[i].astype(jnp.float32), high, share - high):
            out_ref[i, :, at : at + width] = flat(table)
            at += width


def split_kernel(at_ref, group_ref, weight_hbm, *refs):
    parts, sems = refs[:-1], refs[-1]
    chip = at_ref[0] // 2
    sources, targets = [], []
    for k, part in reversed(list(enumerate(parts))):
        for y in range(2):
            start = pl.multiple_of((chip ^ (2 * k + y)) * part.shape[2], LANES)
            rows = pl.ds(pl.multiple_of(group_ref[0] * part.shape[1], 16), part.shape[1])
            sources.append(weight_hbm.at[rows, pl.ds(start, part.shape[2])])
            targets.append(part.at[y])
    for copy in fetch(sources, targets, sems):
        copy.wait()


def regroup_kernel(*refs):
    parts, (_, near_ref, far_ref) = refs[:-3], refs[-3:]
    for k, part in enumerate(parts):
        near_ref[k] = part[0]
        far_ref[k] = part[1]


def position_of(place, per_rows, core):
    return (place // per_rows * 2 + core) * per_rows + place % per_rows


def attend_kernel(
    per_rows,
    at_ref,
    row_ref,
    length_ref,
    key_hbm,
    value_hbm,
    keep_ref,
    send_ref,
    score_ref,
    key_ref,
    value_ref,
    sems,
):
    copies = fetch((key_hbm, value_hbm), (key_ref, value_ref), sems)
    new, heads = row_ref.shape[0], QH // KVH
    wide = heads * HD
    cached = key_ref.shape[0]
    step = math.gcd(cached, 512)
    length = length_ref[:, :1]
    lengths = jnp.concatenate([length] * heads, axis=0)
    query = jnp.concatenate([row_ref[:, h * HD : (h + 1) * HD] for h in range(heads)], axis=0)
    rows = heads * new
    dims = (((1,), (1,)), ((), ()))
    fresh = lax.dot_general(
        query, row_ref[:, wide : wide + HD], dims, preferred_element_type=jnp.float32
    )
    causal = iota((new, new), 1) <= iota((new, new), 0)
    fresh = jnp.where(jnp.concatenate([causal] * heads, axis=0), fresh, -1e30)
    best = jnp.max(fresh, axis=1, keepdims=True)
    peak = jnp.full((rows, LANES), -1e30, jnp.float32)
    copies[0].wait()
    for at in range(0, cached, step):
        part = lax.dot_general(
            query, key_ref[at : at + step, :], dims, preferred_element_type=jnp.float32
        )
        part = jnp.where(iota((rows, step), 1) + at < lengths, part, -1e30)
        score_ref[:, at : at + step] = part
        for lane in range(0, step, LANES):
            peak = jnp.maximum(peak, part[:, lane : lane + LANES])
    best = jnp.maximum(best, jnp.max(peak, axis=1, keepdims=True))
    factor = HD ** (-0.5) * math.log2(math.e)
    fresh = jnp.exp2((fresh - best) * factor)
    sums = jnp.zeros((rows, LANES), jnp.float32)
    for at in range(0, cached, step):
        expo = jnp.exp2((score_ref[:, at : at + step] - best) * factor)
        score_ref[:, at : at + step] = expo
        for lane in range(0, step, LANES):
            sums = sums + expo[:, lane : lane + LANES]
    total = jnp.sum(fresh, axis=1, keepdims=True) + jnp.sum(sums, axis=1, keepdims=True)
    inverse = 1.0 / total
    result = jnp.dot(
        (fresh * inverse).astype(jnp.bfloat16),
        row_ref[:, wide + HD : wide + 2 * HD],
        preferred_element_type=jnp.float32,
    )
    copies[1].wait()
    for at in range(0, cached, step):
        result = result + jnp.dot(
            (score_ref[:, at : at + step] * inverse).astype(jnp.bfloat16),
            value_ref[at : at + step, :],
            preferred_element_type=jnp.float32,
        )
    result = result.astype(jnp.bfloat16)
    result = jnp.concatenate([result[h * new : (h + 1) * new] for h in range(heads)], axis=1)
    half = new // 2
    place = iota((new, new), 0)
    core = (at_ref[0] + place // half) % 2
    pick = iota((new, new), 1) == position_of(place % half, per_rows, core)
    result = jnp.dot(
        pick.astype(jnp.bfloat16), result, preferred_element_type=jnp.float32
    ).astype(jnp.bfloat16)
    keep_ref[...] = result[:half]
    send_ref[...] = result[half:]


def project_kernel(at_ref, group_ref, *refs):
    pieces, columns, (out_ref, weight_ref) = refs[:-10], refs[-10:-2], refs[-2:]
    me = at_ref[0]
    members = len(pieces)
    _, places, wide = pieces[0].shape
    rows = members * places
    part = columns[0].shape[1]
    for i, ref in enumerate(columns):
        for k in range(ref.shape[0]):
            place = 2 * (me ^ (4 * k + i // 2)) + (group_ref[0] ^ (i % 2))
            weight_ref[pl.ds(pl.multiple_of(place * part, part), part), :] = ref[k]
    total = jnp.zeros(out_ref.shape, jnp.float32)
    for half in range(KVH):
        start = pl.multiple_of((me ^ half) % KVH * wide, wide)
        total = total + jnp.dot(
            jnp.concatenate([piece[half] for piece in pieces], axis=0),
            weight_ref[pl.ds(start, wide), :],
            preferred_element_type=jnp.float32,
        )
    token = iota((rows, rows), 0)
    source = ((token % members) ^ (me // KVH)) * places + token // members
    pick = (iota((rows, rows), 1) == source).astype(jnp.bfloat16)
    out_ref[...] = jnp.dot(
        pick, total.astype(jnp.bfloat16), preferred_element_type=jnp.float32
    ).astype(jnp.bfloat16)


def stage_kernel(*refs):
    count = (len(refs) - 1) // 2
    for copy in fetch(refs[:count], refs[count:-1], refs[-1]):
        copy.wait()


def weigh(chip, odd, pieces, gain_ref, *pairs):
    lanes = pieces[0].shape[1]
    starts = [
        pl.multiple_of((chip ^ (2 * i + odd)) * lanes, lanes) for i in range(len(pieces))
    ]
    rows = jnp.concatenate(
        [
            (
                piece[...].astype(jnp.float32)
                * gain_ref[:, pl.ds(start, lanes)].astype(jnp.float32)
            ).astype(jnp.bfloat16)
            for piece, start in zip(pieces, starts)
        ],
        axis=1,
    )

    def part(ref, e):
        return jnp.concatenate([ref[e, pl.ds(start, lanes), :] for start in starts], axis=0)

    return [
        jnp.dot(
            rows,
            jnp.concatenate([part(gate, e), part(up, e)], axis=1),
            preferred_element_type=jnp.float32,
        )
        for gate, up in pairs
        for e in range(gate.shape[0])
    ]


def gate_kernel(at_ref, gain_ref, gate_ref, up_ref, gate_own_ref, up_own_ref, *refs):
    pieces, out_ref = refs[:-1], refs[-1]
    pairs = ((gate_ref, up_ref), (gate_own_ref, up_own_ref))
    for i, value in enumerate(weigh(at_ref[0] // 2, 0, pieces, gain_ref, *pairs)):
        out_ref[i] = value


def block_order(chips):
    near = range(chips - 2, -1, -2)
    return [k + 1 for k in near] + list(near)


def expert_kernel(
    per_rows,
    chips,
    at_ref,
    gain_ref,
    gate_ref,
    up_ref,
    gate_own_ref,
    up_own_ref,
    partial_ref,
    info_ref,
    down_ref,
    down_hbm,
    *refs,
):
    near, far, projected_ref = refs[: chips // 2], refs[chips // 2 : chips], refs[chips]
    outs, result_ref = refs[chips + 1 : -1], refs[-1]
    me = at_ref[0]
    chip, core = me // 2, me % 2
    rows, lanes = near[0].shape
    new = info_ref.shape[0]
    per_dev = rows // chips
    members = per_dev // per_rows
    experts = gate_ref.shape[0]
    width = info_ref.shape[1] // 3

    squares = jnp.zeros((rows, lanes), jnp.float32)
    own = pl.ds(pl.multiple_of(chip * per_dev, per_dev), per_dev)
    for i in range(chips):
        ref = (far if i % 2 else near)[i // 2]
        piece = ref[...].astype(jnp.float32)
        squares = squares + piece * piece
        projected_ref[:, pl.ds(pl.multiple_of((chip ^ i) * lanes, lanes), lanes)] = ref[own, :]
    inverse = lax.rsqrt(jnp.sum(squares, axis=1, keepdims=True) / (chips * lanes) + 1e-06)

    token = iota((rows, new), 0)
    spread = iota((rows, new), 1) == position_of(token // members, per_rows, core)
    info = jnp.dot(
        spread.astype(jnp.bfloat16), info_ref[...], preferred_element_type=jnp.float32
    )
    mine = iota((rows, width), 1) // TOPK == iota((rows, width), 0) % members
    share = jnp.where(mine, info[:, width : 2 * width] + info[:, 2 * width :], 0.0)
    whole = jnp.sum(share, axis=1, keepdims=True)

    pairs = ((gate_ref, up_ref), (gate_own_ref, up_own_ref))
    out = weigh(chip, 1, far, gain_ref, *pairs)
    hidden = []
    for d in range(2 * experts):
        device = me ^ (1 - d // experts)
        chosen = info[:, :width] == (device * experts + d % experts).astype(jnp.float32)
        scale = jnp.sum(jnp.where(chosen, share, 0.0), axis=1, keepdims=True) / whole
        both = (partial_ref[d] + out[d]) * inverse
        gate, up = both[:, : both.shape[1] // 2], both[:, both.shape[1] // 2 :]
        hidden.append((gate / (1.0 + jnp.exp(-gate)) * up * scale).astype(jnp.bfloat16))
    step = 512
    for at in range(0, down_ref.shape[2], step):
        part = jnp.zeros((rows, step), jnp.float32)
        for d, ref in enumerate((down_ref, down_hbm)):
            part = part + jnp.dot(
                jnp.concatenate(hidden[d * experts : (d + 1) * experts], axis=1),
                ref[:, :, at : at + step].reshape(-1, step),
                preferred_element_type=jnp.float32,
            )
        result_ref[:, at : at + step] = part.astype(jnp.bfloat16)
    order = iter(block_order(chips))
    for out in outs:
        for i in range(out.shape[0]):
            start = pl.multiple_of((chip ^ next(order)) * per_dev, per_dev)
            out[i] = result_ref[pl.ds(start, per_dev), :]


def add_kernel(near_ref, piece_ref, *outs):
    for i, out in enumerate(outs):
        out[...] = (
            near_ref[i].astype(jnp.float32) + piece_ref[i].astype(jnp.float32)
        ).astype(jnp.bfloat16)


def sum_kernel(*refs):
    total = refs[0][...].astype(jnp.float32)
    for ref in refs[1:-1]:
        total = total + ref[...].astype(jnp.float32)
    refs[-1][...] = total.astype(jnp.bfloat16)


def swap(value, offset):
    count = lax.axis_size("seq")
    return lax.ppermute(value, "seq", [(i, i ^ offset) for i in range(count)])


def cross(value):
    return lax.ppermute(value, "groups", [(0, 1), (1, 0)])


def scatter_pieces(far, near):
    pieces = []
    ahead = sum(part.shape[0] for part in near)
    for there, here in zip(far, near):
        shape = here.shape[1:]
        sums = call(
            add_kernel, [(shape, jnp.bfloat16)] * here.shape[0], (here, swap(there, 2))
        )
        for piece in sums:
            ahead -= 1
            pieces.append(swap(piece, 4 * ahead) if ahead else piece)
    return pieces


def gather_rows(own):
    count = lax.axis_size("seq")
    near = [own] + [swap(own, k) for k in range(count - 4, 0, -4)][::-1]
    far = [swap(piece, 2) for piece in near]
    return near, far


def exchange_body(
    queries,
    keys,
    values,
    cache_keys,
    cache_values,
    cache_len,
    out_weight,
    norm_gain,
    expert_ids,
    route_weights,
    w_gate,
    w_up,
    w_down,
):
    count = lax.axis_size("seq")
    per_rows, members = queries.shape[0], count // KVH
    new = per_rows * count
    per_dev = per_rows * members
    rows = per_dev * count
    at = lax.axis_index("seq").astype(jnp.int32).reshape(1)
    group = lax.axis_index("groups").astype(jnp.int32).reshape(1)
    width = -(-members * TOPK // LANES) * LANES
    wide = QH // KVH * HD
    bf16 = jnp.bfloat16
    loads = (queries, keys, values, expert_ids, route_weights, cache_len.T)
    sent, seen = call(
        pack_kernel,
        [
            ((per_rows, count, wide + 2 * HD + 3 * width), bf16),
            ((new, LANES), jnp.int32),
        ],
        (*loads, at),
        scratch=[pltpu.VMEM(a.shape, a.dtype) for a in loads] + [pltpu.SemaphoreType.DMA((6,))],
        far=range(6),
    )
    taken = lax.all_to_all(sent, "seq", split_axis=1, concat_axis=0, tiled=True)
    taken = taken.reshape(new, sent.shape[2])
    owned = out_weight.shape[0]
    cached = cache_keys.shape[1]
    chips = count // 2
    lanes = D // chips
    gate_peer, up_peer, down_peer = swap(w_gate, 1), swap(w_up, 1), swap(w_down, 1)
    parts = call(
        split_kernel,
        [((2, owned // 2, lanes), bf16)] * (chips // 2),
        (at, group, out_weight),
        scratch=[pltpu.SemaphoreType.DMA((chips,))],
        far=(2,),
        moved=4 * out_weight.size,
    )
    parts = [parts[0]] + [swap(parts[k], 4 * k) for k in range(len(parts) - 1, 0, -1)][::-1]
    row_count = QH // KVH * new
    keep, send = call(
        functools.partial(attend_kernel, per_rows),
        [((new // 2, wide), bf16)] * 2,
        (at, taken, seen, cache_keys.reshape(cached, HD), cache_values.reshape(cached, HD)),
        scratch=[
            pltpu.VMEM((row_count, cached), jnp.float32),
            pltpu.VMEM((cached, HD), bf16),
            pltpu.VMEM((cached, HD), bf16),
            pltpu.SemaphoreType.DMA((2,)),
        ],
        far=(3, 4),
        flops=4 * row_count * cached * HD,
        moved=4 * cached * HD,
    )
    peer = swap(send, 1)
    own = jnp.stack([keep, peer])
    near, far = gather_rows(own)
    heads = [piece for pair in zip(near, far) for piece in pair]
    columns, across = call(
        regroup_kernel,
        [((chips // 2, owned // 2, lanes), bf16)] * 2,
        (*parts, own),
        loose=(len(parts),),
    )
    beyond = swap(across, 2)
    columns_there = cross(columns)
    own_up, = call(
        stage_kernel,
        [(w_up.shape, bf16)],
        (w_up,),
        scratch=[pltpu.SemaphoreType.DMA((1,))],
        far=range(1),
        vmem_mib=4,
    )
    beyond_there = cross(beyond)
    blocks = [columns, columns_there]
    blocks += [swap(block, 1) for block in blocks]
    blocks += [beyond, beyond_there]
    blocks += [swap(block, 1) for block in blocks[-2:]]
    half = rows // 2
    (projected,) = call(
        project_kernel,
        [((half, lanes), bf16)],
        (at, group, *heads, *blocks),
        scratch=[pltpu.VMEM((D, lanes), bf16)],
        flops=2 * half * D * lanes,
        moved=4 * half * D,
    )
    near, far = gather_rows(projected)
    gain = norm_gain.reshape(1, D)
    experts, _, hidden = w_gate.shape
    (partial,) = call(
        gate_kernel,
        [((2 * experts, half, 2 * hidden), jnp.float32)],
        (at, gain, gate_peer, up_peer, w_gate, own_up, *near),
        vmem_mib=10,
        flops=4 * half * w_gate.size,
        moved=4 * w_gate.size,
    )
    projected, *blocks = call(
        functools.partial(expert_kernel, per_rows, chips),
        [((per_dev, D), bf16)] + [((2, per_dev, D), bf16)] * (chips // 2),
        (
            at,
            gain,
            gate_peer,
            up_peer,
            w_gate,
            own_up,
            partial,
            taken[:, wide + 2 * HD :],
            down_peer,
            w_down,
            *near,
            *far,
        ),
        scratch=[pltpu.VMEM((half, D), bf16)],
        vmem_mib=14,
        flops=8 * half * w_gate.size,
        moved=8 * w_gate.size,
    )
    pieces = scatter_pieces(blocks[: chips // 4], blocks[chips // 4 :])
    (mixed,) = call(sum_kernel, [((per_dev, D), bf16)], pieces)
    shape = (per_rows, members, D)
    return (projected.reshape(shape), mixed.reshape(shape))


def fits(mesh, out_rows, positions, experts):
    count = mesh.shape["seq"]
    owned = out_rows // count
    per_dev = positions // count * (count // KVH)
    pair = mesh.shape["groups"] == 2
    power = count & (count - 1) == 0 and count >= 8
    small = per_dev * count * D * 2 <= 2 << 20
    return pair and power and owned == HD == LANES and count * LANES == D and per_dev % 16 == 0 and positions % 16 == 0 and small and experts <= 256


def attend(query_heads, key_rows, value_rows, lengths):
    new_count = query_heads.shape[0]
    cache_count = key_rows.shape[0] - new_count
    scores = jnp.einsum(
        "qhd,kd->hqk", query_heads, key_rows, preferred_element_type=jnp.float32
    ) * HD ** (-0.5)
    cached_ok = jnp.arange(cache_count, dtype=jnp.int32)[None, :] < lengths[:, None]
    causal_ok = (
        jnp.arange(new_count, dtype=jnp.int32)[None, :]
        <= jnp.arange(new_count, dtype=jnp.int32)[:, None]
    )
    visible = jnp.concatenate([cached_ok, causal_ok], axis=1)
    scores = jnp.where(visible[None], scores, -1e30)
    row_max = jnp.max(scores, axis=-1, keepdims=True)
    expo = jnp.exp(scores - row_max)
    row_sum = jnp.sum(expo, axis=-1, keepdims=True)
    weights = (expo / row_sum).astype(jnp.bfloat16)
    result = jnp.einsum("hqk,kd->qhd", weights, value_rows, preferred_element_type=jnp.float32)
    return result.astype(jnp.bfloat16).reshape(new_count, -1)


def plain_body(
    queries,
    keys,
    values,
    cache_keys,
    cache_values,
    cache_len,
    out_weight,
    norm_gain,
    expert_ids,
    route_weights,
    w_gate,
    own_up,
    w_down,
):
    slot_count = lax.axis_size("seq")
    per_rows = queries.shape[0]
    members = slot_count // KVH
    group_q = QH // KVH
    new_count = per_rows * slot_count
    position_index = lax.axis_index("seq")
    member = position_index // KVH
    query_rows, key_new, value_new = (
        lax.all_to_all(queries, "seq", split_axis=1, concat_axis=0, tiled=True),
        lax.all_to_all(keys, "seq", split_axis=1, concat_axis=0, tiled=True),
        lax.all_to_all(values, "seq", split_axis=1, concat_axis=0, tiled=True),
    )
    key_rows = jnp.concatenate([cache_keys[0], key_new.reshape(new_count, HD)], axis=0)
    value_rows = jnp.concatenate([cache_values[0], value_new.reshape(new_count, HD)], axis=0)
    lengths = lax.dynamic_slice_in_dim(cache_len, member, 1, 1)[:, 0]
    attended = attend(query_rows.reshape(new_count, group_q, HD), key_rows, value_rows, lengths)
    returned_heads = lax.all_to_all(
        attended[:, None, :], "seq", split_axis=0, concat_axis=1, tiled=True
    )
    token_heads = returned_heads.reshape(per_rows * members, QH * HD)
    projected_f = jnp.dot(
        token_heads,
        lax.all_gather(out_weight, "seq", axis=0, tiled=True),
        preferred_element_type=jnp.float32,
    )
    projected_f = projected_f.reshape(per_rows, members, D)
    projected = projected_f.astype(jnp.bfloat16)
    token_count = per_rows * members
    flat_rows = projected.reshape(token_count, D).astype(jnp.float32)
    stats = jnp.mean(flat_rows * flat_rows, axis=-1, keepdims=True)
    normed = (flat_rows * lax.rsqrt(stats + 1e-06) * norm_gain.astype(jnp.float32)).astype(
        jnp.bfloat16
    )
    exp_dev = w_gate.shape[0]
    expert_count = exp_dev * slot_count
    chosen_ids = expert_ids.reshape(token_count * TOPK)
    onehot = (chosen_ids[:, None] == jnp.arange(expert_count, dtype=jnp.int32)[None, :]).astype(
        jnp.int32
    )
    slot_rank = jnp.sum((jnp.cumsum(onehot, axis=0) - onehot) * onehot, axis=1)
    owner = chosen_ids // exp_dev
    local_expert = chosen_ids % exp_dev
    slot_target = (local_expert * slot_count + owner) * CAP + slot_rank
    total_slots = exp_dev * slot_count * CAP
    token_of = jnp.arange(token_count * TOPK, dtype=jnp.int32) // TOPK
    source_row = jnp.full((total_slots,), -1, jnp.int32).at[slot_target].set(token_of)
    filled = source_row >= 0
    outgoing = jnp.where(
        filled[:, None], normed[jnp.maximum(source_row, 0)], jnp.zeros((), jnp.bfloat16)
    )
    outgoing = outgoing.reshape(exp_dev, slot_count, CAP, D)
    incoming = lax.all_to_all(outgoing, "seq", split_axis=1, concat_axis=1, tiled=True)
    row_block = incoming.reshape(exp_dev, slot_count * CAP, D)
    gate_out = jnp.einsum("ecd,edf->ecf", row_block, w_gate, preferred_element_type=jnp.float32)
    up_out = jnp.einsum("ecd,edf->ecf", row_block, own_up, preferred_element_type=jnp.float32)
    hidden_act = (jax.nn.silu(gate_out) * up_out).astype(jnp.bfloat16)
    expert_out = jnp.einsum(
        "ecf,efd->ecd", hidden_act, w_down, preferred_element_type=jnp.float32
    ).astype(jnp.bfloat16)
    expert_back = lax.all_to_all(
        expert_out.reshape(exp_dev, slot_count, CAP, D),
        "seq",
        split_axis=1,
        concat_axis=1,
        tiled=True,
    )
    picked = expert_back.reshape(total_slots, D)[slot_target].reshape(token_count, TOPK, D)
    raw_weights = route_weights.reshape(token_count, TOPK)
    norm_weights = raw_weights / jnp.sum(raw_weights, axis=1, keepdims=True)
    mixed = jnp.sum(norm_weights[:, :, None] * picked.astype(jnp.float32), axis=1)
    moe_out = mixed.astype(jnp.bfloat16).reshape(per_rows, members, D)
    return (projected, moe_out)


def solution(mesh):
    def run(*args):
        exchanged = fits(mesh, args[6].shape[0], args[0].shape[0], args[10].shape[0])
        step = jax.shard_map(
            exchange_body if exchanged else plain_body,
            mesh=mesh,
            in_specs=(
                P("seq", "groups", None),
                P("seq", "groups", None),
                P("seq", "groups", None),
                P(("groups", "seq"), None, None),
                P(("groups", "seq"), None, None),
                P(None, "groups"),
                P("seq", None),
                P(),
                P("seq", "groups", None),
                P("seq", "groups", None),
                P("seq", None, None),
                P("seq", None, None),
                P("seq", None, None),
            ),
            out_specs=(P("seq", "groups", None), P("seq", "groups", None)),
            check_vma=False,
        )
        return step(*args)

    return run
```
